32 devices in a mesh: grp: 4 (over x, core), tok: 8 (over z, y).
Axes of the slice: x: 2, y: 2, z: 4, core: 2. Of those that a mesh axis runs over, the one named last changes fastest.
Arguments:
- layer_input: bfloat16 [32768, 768], P(('grp', 'tok')), may hold values from -6 to 6
- doc_starts: int32 [32768], P(('grp', 'tok')), may hold values 0 or 1
- ln1_gain: float32 [768], replicated, may hold values from 0.5 to 1.5
- ln1_shift: float32 [768], replicated, may hold values from -3 to 3
- w_qkv: bfloat16 [768, 2304], replicated, may hold values from -0.21875 to 0.21875
- feat_q: bfloat16 [768, 64], replicated, may hold values from -0.75 to 0.75
- feat_k: bfloat16 [768, 64], replicated, may hold values from -0.75 to 0.75
- w_out: bfloat16 [768, 768], replicated, may hold values from -6 to 6
- ln2_gain: float32 [768], replicated, may hold values from 0.5 to 1.5
- ln2_shift: float32 [768], replicated, may hold values from -3 to 3
- w_fc: bfloat16 [768, 3072], replicated, may hold values from -0.21875 to 0.21875
- w_proj: bfloat16 [3072, 768], replicated, may hold values from -0.109375 to 0.109375
- cotangent: bfloat16 [32768, 768], P(('grp', 'tok')), may hold values from -6 to 6
Outputs:
- output: bfloat16 [32768, 768], P(('grp', 'tok'))
- grad_input: float32 [32768, 768], P(('grp', 'tok'))
- grad_ln1_gain: float32 [768], P('tok')
- grad_ln1_shift: float32 [768], P('tok')
- grad_qkv: float32 [768, 2304], P('tok')
- grad_feat_q: float32 [768, 64], P('tok')
- grad_feat_k: float32 [768, 64], P('tok')
- grad_w_out: float32 [768, 768], P('tok')
- grad_ln2_gain: float32 [768], P('tok')
- grad_ln2_shift: float32 [768], P('tok')
- grad_fc: float32 [768, 3072], P('tok')
- grad_proj: float32 [3072, 768], P('tok')
The draws below stay inside these ranges and needn't reach their ends.
Inputs may be any that keep to these rules, and one draw needn't show every extreme that they name: `doc_starts`: 1 marks the first token of a document; attention and carried sums stop there.
All inputs are finite; a program needn't handle non-finite values. No bound on the sum of `doc_starts` on one device may be relied on, other than what follows from the above.
Results may differ from the reference program's by a relative error of at most 0.011.
Values sent between devices are 32-bit elements; how exact they have to be, the bound alone decides.
No kernel may reach another device: no remote copies, remote signals or barrier semaphores. Data moves between devices by JAX's collectives and lax.ppermute only.
A program may use at most 768 MiB of HBM per device.

```python
import jax
import jax.numpy as jnp
from jax import lax

D = 768
H = 12
HD = 64
FF = 3072
FEAT = 128
TOK_DEV = 1024
TOKENS = 32768


def place_ends(array, key, least, largest):
    longest = array.shape.index(max(array.shape))
    spots = []
    for shift in (0, 1):
        where = [jax.random.randint(jax.random.fold_in(key, axis), (), 0, length) for axis, length in enumerate(array.shape)]
        where[longest] = (where[longest] + shift) % array.shape[longest]
        spots.append(tuple(where))
    return array.at[spots[0]].set(least).at[spots[1]].set(largest)


def spiked(values, rng, source, target, parts, factor):
    def block_of(axis_at):
        return (jnp.arange(values.shape[axis_at]) // (values.shape[axis_at] // parts)).reshape((-1,) + (1,) * (values.ndim - 1 - axis_at))

    first = jax.random.permutation(rng, parts)[block_of(target)]
    second = (block_of(target) + parts // 2) % parts
    return jnp.where((block_of(source) == first) | (block_of(source) == second), factor * values, values)


def steps_of(rng, shape, split, low, top_value):
    def one(axis_at, shards_of):
        steps = jax.random.uniform(jax.random.fold_in(jax.random.fold_in(rng, 6), axis_at), (shards_of,), jnp.float32, low / len(split), top_value / len(split))
        return jnp.repeat(jnp.exp(steps), shape[axis_at] // shards_of).reshape((-1,) + (1,) * (len(shape) - axis_at - 1))

    level = one(*split[0])
    for cut in split[1:]:
        level = level * one(*cut)
    return level


def noise(key, extent, width, most, cuts=(), kind=jnp.bfloat16):
    entries = width * jax.random.normal(key, extent, jnp.float32)
    if cuts:
        entries = entries * steps_of(key, extent, cuts, -0.22, 0.18)
    return jnp.clip(entries, -most, most).astype(kind)


def gaussian_with(rng, shape, spread, bound, pieces, heavy, dtype=jnp.bfloat16):
    values = spread * jax.random.normal(rng, shape, jnp.float32)
    if pieces:
        values = values * steps_of(rng, shape, pieces, -0.22, 0.18)
    return jnp.clip(spiked(values, jax.random.fold_in(rng, 3), *heavy), -bound, bound).astype(dtype)


def setup_inputs(seed: int = 0) -> dict:
    seeds = jax.random.split(jax.random.key(seed), 14)
    return {
        "layer_input": gaussian_with(seeds[0], (TOKENS, D), 1.0, 6.0, ((0, 32),), (0, 1, 32, 2.75)),
        "doc_starts": place_ends((jax.random.randint(seeds[1], (TOKENS,), 0, 4 * TOK_DEV) < 1).astype(jnp.int32), jax.random.fold_in(seeds[1], 1), 0, 1),
        "ln1_gain": jnp.clip(1.0 + 0.1 * jax.random.normal(seeds[2], (D,), jnp.float32), 0.5, 1.5),
        "ln1_shift": noise(seeds[3], (D,), 0.3, 3.0, (), jnp.float32),
        "w_qkv": noise(seeds[4], (D, 3 * D), D ** -0.5, 0.21875),
        "feat_q": noise(seeds[5], (D, HD), HD ** -0.5, 0.75),
        "feat_k": noise(seeds[6], (D, HD), HD ** -0.5, 0.75),
        "w_out": noise(seeds[7], (D, D), (max(D // (4 * TOK_DEV), 1)) ** -0.5, 6.0),
        "ln2_gain": jnp.clip(1.0 + 0.1 * jax.random.normal(seeds[8], (D,), jnp.float32), 0.5, 1.5),
        "ln2_shift": noise(seeds[9], (D,), 0.3, 3.0, (), jnp.float32),
        "w_fc": noise(seeds[10], (D, FF), D ** -0.5, 0.21875),
        "w_proj": noise(seeds[11], (FF, D), FF ** -0.5, 0.109375),
        "cotangent": noise(seeds[12], (TOKENS, D), 1.0, 6.0, ((0, 32),)),
    }


@jax.custom_vjp
def low(v):
    return lax.optimization_barrier(v.astype(jnp.bfloat16)).astype(jnp.float32)

@jax.custom_vjp
def low_back(v):
    return v

def low_keep(v):
    return (low(v), None)

def low_pass(kept, grad):
    return (grad,)

def back_keep(v):
    return (v, None)

def back_low(kept, grad):
    return (low(grad),)
low.defvjp(low_keep, low_pass)
low_back.defvjp(back_keep, back_low)
eps = 1e-05
highest = lax.Precision.HIGHEST

def layer_norm(value, gain, shift):
    centre = lax.optimization_barrier(jnp.mean(value, axis=-1, keepdims=True))
    centered = value - centre
    variance = lax.optimization_barrier(jnp.mean(centered * centered, axis=-1, keepdims=True))
    return centered * lax.rsqrt(variance + eps) * gain + shift

def feature_map(logits):
    return jnp.concatenate([jax.nn.softmax(logits, axis=-1), jax.nn.softmax(-logits, axis=-1)], axis=-1)

def attend_block(carry_pair, inputs):
    carry_state, normer = carry_pair
    query_feat, key_feat, values, starts = inputs
    block_len = query_feat.shape[0]
    segment = jnp.cumsum(starts)
    position = jnp.arange(block_len)
    allowed = (position[:, None] >= position[None, :]) & (segment[:, None] == segment[None, :])
    opened = (segment == 0.0).astype(jnp.float32)
    closing = (segment == segment[-1]).astype(jnp.float32)
    scores = jnp.einsum('thf,shf->hts', query_feat, key_feat, precision=highest)
    weights = low_back(low(jnp.where(allowed[None], scores, 0.0)))
    numer_local = low_back(jnp.einsum('hts,shd->thd', weights, values, precision=highest))
    numer_carry = opened[:, None, None] * jnp.einsum('thf,hfd->thd', query_feat, carry_state, precision=highest)
    denominator = lax.optimization_barrier(jnp.sum(weights, axis=2)).T + opened[:, None] * jnp.einsum('thf,hf->th', query_feat, normer, precision=highest)
    mixed_out = (numer_local + numer_carry) / denominator[:, :, None]
    tail_keys = key_feat * closing[:, None, None]
    reset_flag = jnp.minimum(segment[-1], 1.0)
    state_next = jnp.einsum('shf,shd->hfd', tail_keys, values, precision=highest) + (1.0 - reset_flag) * carry_state
    normer_next = lax.optimization_barrier(jnp.sum(tail_keys, axis=0)) + (1.0 - reset_flag) * normer
    return ((state_next, normer_next), mixed_out)

def forward(flags_float, inputs, ln1_gain, ln1_shift, w_qkv, feat_q, feat_k, w_out, ln2_gain, ln2_shift, w_fc, w_proj):
    tokens = inputs.shape[0]
    hidden1 = low(layer_norm(inputs, ln1_gain, ln1_shift))
    packed = low_back(low(jnp.dot(hidden1, w_qkv, precision=highest)))
    queries = packed[:, :D].reshape(tokens, H, HD)
    key_vals = packed[:, D:2 * D].reshape(tokens, H, HD)
    values = packed[:, 2 * D:].reshape(tokens, H, HD)
    logit_query = low_back(jnp.einsum('thi,hij->thj', queries, feat_q.reshape(H, HD, HD), precision=highest))
    logit_key = low_back(jnp.einsum('thi,hij->thj', key_vals, feat_k.reshape(H, HD, HD), precision=highest))
    phi_query = low(feature_map(logit_query))
    phi_key = low(feature_map(logit_key))
    blocks = tokens // TOK_DEV
    initial = (jnp.zeros((H, FEAT, HD), jnp.float32), jnp.zeros((H, FEAT), jnp.float32))
    scanned = (phi_query.reshape(blocks, TOK_DEV, H, FEAT), phi_key.reshape(blocks, TOK_DEV, H, FEAT), values.reshape(blocks, TOK_DEV, H, HD), flags_float.reshape(blocks, TOK_DEV))
    _, mixed_out = lax.scan(jax.checkpoint(attend_block), initial, scanned)
    mixed_low = low(mixed_out.reshape(tokens, D))
    branch = low_back(jnp.dot(mixed_low, w_out, precision=highest))
    resid = inputs + branch
    hidden2 = low(layer_norm(resid, ln2_gain, ln2_shift))
    pre_act = low_back(jnp.dot(hidden2, w_fc, precision=highest))
    act_low = low(jax.nn.gelu(pre_act, approximate=True))
    return resid + jnp.dot(act_low, w_proj, precision=highest)

def reference(layer_input, doc_starts, ln1_gain, ln1_shift, w_qkv, feat_q, feat_k, w_out, ln2_gain, ln2_shift, w_fc, w_proj, cotangent):
    flags_float = doc_starts.astype(jnp.float32)

    def layer_fn(inputs, gain_one, shift_one, mat_qkv, maps_q, maps_k, mat_out, gain_two, shift_two, mat_fc, mat_proj):
        return forward(flags_float, inputs, gain_one, shift_one, mat_qkv, maps_q, maps_k, mat_out, gain_two, shift_two, mat_fc, mat_proj)
    result, pullback = jax.vjp(layer_fn, layer_input.astype(jnp.float32), ln1_gain.astype(jnp.float32), ln1_shift.astype(jnp.float32), w_qkv.astype(jnp.float32), feat_q.astype(jnp.float32), feat_k.astype(jnp.float32), w_out.astype(jnp.float32), ln2_gain.astype(jnp.float32), ln2_shift.astype(jnp.float32), w_fc.astype(jnp.float32), w_proj.astype(jnp.float32))
    grads = pullback(cotangent.astype(jnp.float32))
    return (result.astype(jnp.bfloat16), grads[0], grads[1], grads[2], grads[3], grads[4], grads[5], grads[6], grads[7], grads[8], grads[9], grads[10])
```

```python
from functools import partial

import jax
import jax.numpy as jnp
from jax import lax
from jax.sharding import PartitionSpec as P

eps = 1e-05
highest = lax.Precision.HIGHEST


def log2_of(count):
    return count.bit_length() - 1


def flips(grp_size, tok_size, first, second):
    pairs = []
    for place in range(grp_size * tok_size):
        grp = place // tok_size
        pairs.append((place, place ^ (second if grp % 2 else first)))
    return pairs


def carry_scan(packed, keep, backward):
    grp_size, tok_size = (lax.axis_size("grp"), lax.axis_size("tok"))
    place = lax.axis_index("grp") * tok_size + lax.axis_index("tok")
    rows = packed.shape[0]
    total = jnp.concatenate([packed, jnp.full((4, 128), keep, jnp.float32)], axis=0)
    is_keep = lax.broadcasted_iota(jnp.int32, total.shape, 0) >= rows
    prefix = jnp.where(is_keep, 1.0, 0.0)
    steps = log2_of(grp_size * tok_size)
    for step in range(steps):
        other = lax.ppermute(total, ("grp", "tok"), flips(grp_size, tok_size, 1 << step, 1 << step))
        bit = (place >> step) & 1
        later = (bit == 0) if backward else (bit == 1)
        prefix = jnp.where(later, jnp.where(is_keep, 0.0, prefix) + prefix[rows, 0] * other, prefix)
        if step + 1 < steps:
            late = jnp.where(later, total, other)
            early = jnp.where(later, other, total)
            total = jnp.where(is_keep, 0.0, late) + late[rows, 0] * early
    return prefix[:rows]


def reduce_rows(grad):
    grp_size, tok_size = (lax.axis_size("grp"), lax.axis_size("tok"))
    axes = ("grp", "tok")
    core = lax.axis_index("grp") % 2
    place = lax.axis_index("grp") * tok_size + lax.axis_index("tok")
    tok_bits, far_bits = (log2_of(tok_size), log2_of(grp_size) - 1)
    width = grad.shape[1]
    rows = grad.shape[0] // tok_size
    sub = rows // grp_size
    far = grp_size // 2
    view = grad.reshape(tok_size, 2, far * sub, width)
    mine = lax.dynamic_index_in_dim(view, core, 1, keepdims=False)
    theirs = lax.dynamic_index_in_dim(view, 1 - core, 1, keepdims=False)
    mine = mine + lax.ppermute(theirs, axes, flips(grp_size, tok_size, tok_size, tok_size))
    dims = (2,) * (tok_bits + far_bits)
    mine = mine.reshape(dims + (sub, width))
    tok_axes = list(range(tok_bits))[::-1]
    far_axes = [tok_bits + i for i in range(far_bits)][::-1]
    order_a = far_axes + tok_axes
    order_b = tok_axes + far_axes
    tail = (len(dims), len(dims) + 1)
    buf = jnp.where(
        core == 0,
        mine.transpose(*order_a, *tail),
        mine.transpose(*order_b, *tail),
    ).reshape(-1, sub, width)
    tok_flips = [1 << i for i in range(tok_bits)]
    far_flips = [(2 * tok_size) << i for i in range(far_bits)]
    flips_a = far_flips + tok_flips
    flips_b = tok_flips + far_flips
    for flip_a, flip_b in zip(flips_a, flips_b):
        bit = jnp.where(core == 0, (place & flip_a) != 0, (place & flip_b) != 0).astype(jnp.int32)
        half = buf.shape[0] // 2
        keep = lax.dynamic_slice_in_dim(buf, bit * half, half, 0)
        give = lax.dynamic_slice_in_dim(buf, (1 - bit) * half, half, 0)
        buf = keep + lax.ppermute(give, axes, flips(grp_size, tok_size, flip_a, flip_b))
    for flip in far_flips + [tok_size]:
        bit = (place & flip) != 0
        other = lax.ppermute(buf, axes, flips(grp_size, tok_size, flip, flip))
        buf = jnp.concatenate(
            [jnp.where(bit, other, buf), jnp.where(bit, buf, other)], axis=0
        )
    return buf.reshape(rows, width)


def reduce_vectors(stack):
    grp_size, tok_size = (lax.axis_size("grp"), lax.axis_size("tok"))
    count, length = stack.shape
    share = length // tok_size
    blocks = stack.reshape(count, tok_size, share).transpose(1, 0, 2)
    blocks = blocks.reshape(tok_size, count * share)
    spread = jnp.broadcast_to(blocks[None], (grp_size,) + blocks.shape)
    spread = spread.reshape(grp_size * tok_size, count * share)
    landed = lax.all_to_all(spread, ("grp", "tok"), 0, 0, tiled=True)
    return jnp.sum(landed, axis=0).reshape(count, share)


def layer_norm(value, gain, shift):
    centre = jnp.mean(value, axis=-1, keepdims=True)
    centered = value - centre
    variance = jnp.mean(centered * centered, axis=-1, keepdims=True)
    return centered * lax.rsqrt(variance + eps) * gain + shift


def feature_map(logits):
    return jnp.concatenate(
        [jax.nn.softmax(logits, axis=-1), jax.nn.softmax(-logits, axis=-1)], axis=-1
    )


def on_device(
    layer_input,
    doc_starts,
    ln1_gain,
    ln1_shift,
    w_qkv,
    feat_q,
    feat_k,
    w_out,
    ln2_gain,
    ln2_shift,
    w_fc,
    w_proj,
    cotangent,
):
    tokens, model_width = layer_input.shape
    head_dim = feat_q.shape[1]
    head_count = model_width // head_dim
    block_rows = min(512, tokens)
    xfloat = layer_input.astype(jnp.float32)
    normed1, ln1_back = jax.vjp(layer_norm, xfloat, ln1_gain, ln1_shift)
    hidden1 = normed1.astype(jnp.bfloat16)
    packed = jnp.dot(hidden1, w_qkv, preferred_element_type=jnp.float32).astype(jnp.bfloat16)
    queries = packed[:, :model_width].reshape(tokens, head_count, head_dim)
    key_vals = packed[:, model_width : 2 * model_width].reshape(tokens, head_count, head_dim)
    values = packed[:, 2 * model_width :].reshape(tokens, head_count, head_dim)
    maps_query = feat_q.reshape(head_count, head_dim, head_dim)
    maps_key = feat_k.reshape(head_count, head_dim, head_dim)
    logit_query = jnp.einsum(
        "thi,hij->thj", queries, maps_query, preferred_element_type=jnp.float32
    )
    logit_key = jnp.einsum("thi,hij->thj", key_vals, maps_key, preferred_element_type=jnp.float32)
    feat_query, query_back = jax.vjp(feature_map, logit_query)
    feat_key, key_back = jax.vjp(feature_map, logit_key)
    phi_query = feat_query.astype(jnp.bfloat16)
    phi_key = feat_key.astype(jnp.bfloat16)
    segment = jnp.cumsum(doc_starts)
    position = jnp.arange(tokens)
    opened = (segment == 0).astype(jnp.float32)
    closing = segment == segment[-1]
    reset_flag = jnp.minimum(segment[-1], 1).astype(jnp.float32)
    tail_keys = jnp.where(closing[:, None, None], phi_key, jnp.zeros_like(phi_key))
    state_local = jnp.einsum("shf,shd->hfd", tail_keys, values, preferred_element_type=jnp.float32)
    normer_local = jnp.sum(tail_keys, axis=0, dtype=jnp.float32)
    def pack(state, normer):
        return jnp.concatenate(
            [state.transpose(0, 2, 1).reshape(model_width, 2 * head_dim), normer], axis=0
        )

    def unpack(packed):
        state = packed[:model_width].reshape(head_count, head_dim, 2 * head_dim)
        return state.transpose(0, 2, 1), packed[model_width:]

    state_in, normer_in = unpack(carry_scan(pack(state_local, normer_local), 1.0 - reset_flag, False))

    def block_weights(offset):
        scores = jnp.einsum(
            "thf,shf->hts",
            phi_query[offset : offset + block_rows],
            phi_key,
            preferred_element_type=jnp.float32,
        )
        allowed = (position[offset : offset + block_rows, None] >= position[None, :]) & (
            segment[offset : offset + block_rows, None] == segment[None, :]
        )
        return (allowed, jnp.where(allowed[None], scores, 0.0).astype(jnp.bfloat16))

    mixed_parts = []
    denom_parts = []
    for offset in range(0, tokens, block_rows):
        allowed, weights = block_weights(offset)
        open_rows = opened[offset : offset + block_rows]
        query_wide = phi_query[offset : offset + block_rows].astype(jnp.float32)
        numer_local = jnp.einsum(
            "hts,shd->thd", weights, values, preferred_element_type=jnp.float32
        )
        numer_carry = open_rows[:, None, None] * jnp.einsum(
            "thf,hfd->thd", query_wide, state_in, precision=highest
        )
        denominator = jnp.sum(weights, axis=2, dtype=jnp.float32).T + open_rows[
            :, None
        ] * jnp.einsum("thf,hf->th", query_wide, normer_in, precision=highest)
        mixed_parts.append((numer_local + numer_carry) / denominator[:, :, None])
        denom_parts.append(denominator)
    mixed_all = jnp.concatenate(mixed_parts, axis=0)
    denom_all = jnp.concatenate(denom_parts, axis=0)
    mixed_low = mixed_all.reshape(tokens, model_width).astype(jnp.bfloat16)
    resid = xfloat + jnp.dot(mixed_low, w_out, preferred_element_type=jnp.float32)
    normed2, ln2_back = jax.vjp(layer_norm, resid, ln2_gain, ln2_shift)
    hidden2 = normed2.astype(jnp.bfloat16)
    pre_act = jnp.dot(hidden2, w_fc, preferred_element_type=jnp.float32)
    activ, gelu_back = jax.vjp(partial(jax.nn.gelu, approximate=True), pre_act)
    act_low = activ.astype(jnp.bfloat16)
    output = (resid + jnp.dot(act_low, w_proj, preferred_element_type=jnp.float32)).astype(
        jnp.bfloat16
    )
    grad_proj = jnp.dot(act_low.T, cotangent, preferred_element_type=jnp.float32)
    dact = jnp.dot(cotangent, w_proj.T, preferred_element_type=jnp.float32)
    dpre = gelu_back(dact)[0].astype(jnp.bfloat16)
    grad_fc = jnp.dot(hidden2.T, dpre, preferred_element_type=jnp.float32)
    dhidden2 = jnp.dot(dpre, w_fc.T, preferred_element_type=jnp.float32)
    dresid_norm, grad_g2, grad_b2 = ln2_back(dhidden2)
    dresid = cotangent.astype(jnp.float32) + dresid_norm
    dbranch = dresid.astype(jnp.bfloat16)
    grad_out = jnp.dot(mixed_low.T, dbranch, preferred_element_type=jnp.float32)
    dmixed = jnp.dot(dbranch, w_out.T, preferred_element_type=jnp.float32).reshape(
        tokens, head_count, head_dim
    )
    grad_phiq_parts = []
    grad_phik = jnp.zeros((tokens, head_count, 2 * head_dim), jnp.float32)
    grad_values = jnp.zeros((tokens, head_count, head_dim), jnp.float32)
    grad_state = jnp.zeros_like(state_local)
    grad_normer = jnp.zeros_like(normer_local)
    for offset in range(0, tokens, block_rows):
        allowed, weights = block_weights(offset)
        open_rows = opened[offset : offset + block_rows]
        query_rows = phi_query[offset : offset + block_rows]
        query_wide = query_rows.astype(jnp.float32)
        denominator = denom_all[offset : offset + block_rows]
        dmixed_rows = dmixed[offset : offset + block_rows]
        dnumer = dmixed_rows / denominator[:, :, None]
        ddenom = (
            -jnp.sum(dmixed_rows * mixed_all[offset : offset + block_rows], axis=2) / denominator
        )
        dnumer_low = dnumer.astype(jnp.bfloat16)
        dweights = (
            jnp.einsum("thd,shd->hts", dnumer_low, values, preferred_element_type=jnp.float32)
            + ddenom.T[:, :, None]
        )
        dweights = jnp.where(allowed[None], dweights, 0.0).astype(jnp.bfloat16)
        grad_query = jnp.einsum(
            "hts,shf->thf", dweights, phi_key, preferred_element_type=jnp.float32
        )
        grad_query = grad_query + open_rows[:, None, None] * (
            jnp.einsum("thd,hfd->thf", dnumer, state_in, precision=highest)
            + ddenom[:, :, None] * normer_in[None]
        )
        grad_phiq_parts.append(grad_query)
        grad_phik = grad_phik + jnp.einsum(
            "hts,thf->shf", dweights, query_rows, preferred_element_type=jnp.float32
        )
        grad_values = grad_values + jnp.einsum(
            "hts,thd->shd", weights, dnumer_low, preferred_element_type=jnp.float32
        )
        open_query = query_wide * open_rows[:, None, None]
        grad_state = grad_state + jnp.einsum("thf,thd->hfd", open_query, dnumer, precision=highest)
        grad_normer = grad_normer + jnp.einsum("th,thf->hf", ddenom, open_query, precision=highest)
    back_state, back_normer = unpack(
        carry_scan(pack(grad_state, grad_normer), 1.0 - reset_flag, True)
    )
    closing_wide = closing.astype(jnp.float32)[:, None, None]
    grad_phik = grad_phik + closing_wide * (
        jnp.einsum("shd,hfd->shf", values.astype(jnp.float32), back_state, precision=highest)
        + back_normer[None]
    )
    grad_values = grad_values + closing_wide * jnp.einsum(
        "shf,hfd->shd", phi_key.astype(jnp.float32), back_state, precision=highest
    )
    grad_phiq = jnp.concatenate(grad_phiq_parts, axis=0)
    dlogit_query = query_back(grad_phiq)[0].astype(jnp.bfloat16)
    dlogit_key = key_back(grad_phik)[0].astype(jnp.bfloat16)
    grad_featq = jnp.einsum(
        "thi,thj->hij", queries, dlogit_query, preferred_element_type=jnp.float32
    ).reshape(model_width, head_dim)
    grad_featk = jnp.einsum(
        "thi,thj->hij", key_vals, dlogit_key, preferred_element_type=jnp.float32
    ).reshape(model_width, head_dim)
    dqueries = jnp.einsum(
        "thj,hij->thi", dlogit_query, maps_query, preferred_element_type=jnp.float32
    )
    dkeys = jnp.einsum("thj,hij->thi", dlogit_key, maps_key, preferred_element_type=jnp.float32)
    dpacked = jnp.concatenate(
        [
            dqueries.reshape(tokens, model_width),
            dkeys.reshape(tokens, model_width),
            grad_values.reshape(tokens, model_width),
        ],
        axis=1,
    ).astype(jnp.bfloat16)
    grad_qkv = jnp.dot(hidden1.T, dpacked, preferred_element_type=jnp.float32)
    dhidden1 = jnp.dot(dpacked, w_qkv.T, preferred_element_type=jnp.float32)
    dx_norm, grad_g1, grad_b1 = ln1_back(dhidden1)
    grad_input = dresid + dx_norm
    vectors = reduce_vectors(jnp.stack([grad_g1, grad_b1, grad_g2, grad_b2]))
    share_feat = reduce_rows(jnp.concatenate([grad_featq, grad_featk], axis=1))
    return (
        output,
        grad_input,
        vectors[0],
        vectors[1],
        reduce_rows(grad_qkv),
        share_feat[:, :head_dim],
        share_feat[:, head_dim:],
        reduce_rows(grad_out),
        vectors[2],
        vectors[3],
        reduce_rows(grad_fc),
        reduce_rows(grad_proj),
    )


def solution(mesh):
    in_specs = (
        P(("grp", "tok"), None),
        P(("grp", "tok")),
        P(),
        P(),
        P(),
        P(),
        P(),
        P(),
        P(),
        P(),
        P(),
        P(),
        P(("grp", "tok"), None),
    )
    out_specs = (
        P(("grp", "tok"), None),
        P(("grp", "tok"), None),
        P("tok"),
        P("tok"),
        P("tok", None),
        P("tok", None),
        P("tok", None),
        P("tok", None),
        P("tok"),
        P("tok"),
        P("tok", None),
        P("tok", None),
    )
    return jax.shard_map(
        on_device, mesh=mesh, in_specs=in_specs, out_specs=out_specs, check_vma=False
    )
```

```python
import jax
import jax.numpy as jnp
from jax import lax
from jax.experimental import pallas as pl
from jax.experimental.pallas import tpu as pltpu
from jax.sharding import PartitionSpec as P

eps = 1e-05
f32 = jnp.float32
bf16 = jnp.bfloat16
grant = 56 * 1024 * 1024


def dg(left, right, left_dim, right_dim):
    dims = (((left_dim,), (right_dim,)), ((), ()))
    return lax.dot_general(left, right, dims, preferred_element_type=f32)


def parts_of(value):
    high = value.astype(bf16).astype(f32)
    return high, value - high


def rows_of(rows, width):
    at = lax.broadcasted_iota(jnp.int32, (16, width), 0)
    block = jnp.zeros((16, width), f32)
    for place, row in enumerate(rows):
        block = jnp.where(at == place, row, block)
    return block


def stacked(*blocks):
    return jnp.concatenate([block.astype(bf16) for block in blocks], axis=0)


def norm_parts(value):
    centered = value - jnp.mean(value, axis=1, keepdims=True)
    variance = jnp.mean(centered * centered, axis=1, keepdims=True)
    scale = lax.rsqrt(variance + eps)
    return centered * scale, scale


def norm_back(unit, scale, gain, grad):
    scaled = grad * gain
    along = jnp.mean(scaled * unit, axis=1, keepdims=True)
    return scale * (scaled - jnp.mean(scaled, axis=1, keepdims=True) - unit * along)


def enter_kernel(
    x_ref, gain_ref, shift_ref, w_ref, fq_ref, fk_ref, tail_ref,
    hid_ref, qkv_ref, pq_ref, pk_ref, state_ref, norm_ref,
):
    width, head_dim = fq_ref.shape
    rows = x_ref.shape[0]
    unit, _ = norm_parts(x_ref[...].astype(f32))
    hid = (unit * gain_ref[...] + shift_ref[...]).astype(bf16)
    hid_ref[...] = hid
    qkv_ref[...] = dg(w_ref[...], hid, 0, 1).astype(bf16)

    @pl.when(pl.program_id(0) == 0)
    def _():
        state_ref[...] = jnp.zeros_like(state_ref)
        norm_ref[...] = jnp.zeros_like(norm_ref)

    def features(maps, token_rows):
        logits = dg(maps, token_rows, 0, 0)
        up = jnp.exp(logits - jnp.max(logits, axis=0, keepdims=True))
        down = jnp.exp(jnp.min(logits, axis=0, keepdims=True) - logits)
        up = up / jnp.sum(up, axis=0, keepdims=True)
        down = down / jnp.sum(down, axis=0, keepdims=True)
        return stacked(up, down)

    ones = jnp.ones((16, rows), bf16)
    for head in range(width // head_dim):
        low, high = (head * head_dim, (head + 1) * head_dim)
        pq_ref[2 * low : 2 * high, :] = features(fq_ref[low:high, :], qkv_ref[low:high, :])
        phi = features(fk_ref[low:high, :], qkv_ref[width + low : width + high, :])
        pk_ref[2 * low : 2 * high, :] = phi
        wide = stacked(qkv_ref[2 * width + low : 2 * width + high, :], ones)
        local = dg(wide, phi * tail_ref[...], 1, 1)
        state_ref[low:high, :] += local[:head_dim]
        norm_ref[head : head + 1, :] += local[head_dim : head_dim + 1]


def masked(scores, start, offset):
    key_at = lax.broadcasted_iota(jnp.int32, scores.shape, 0)
    query_at = lax.broadcasted_iota(jnp.int32, scores.shape, 1) + offset
    allowed = (key_at >= start) & (key_at <= query_at)
    return jnp.where(allowed, scores, 0.0).astype(bf16)


def local_kernel(pq_ref, pk_ref, v_ref, start_ref, num_ref, den_ref):
    tokens = pq_ref.shape[1]
    head_dim = v_ref.shape[0]
    step = min(256, tokens)
    for low in range(0, tokens, step):
        high = low + step
        scores = dg(pk_ref[:, :high], pq_ref[:, low:high], 0, 0)
        weights = masked(scores, start_ref[:, low:high], low)
        wide = stacked(v_ref[:, :high], jnp.ones((16, high), bf16))
        local = dg(wide, weights, 1, 0)
        num_ref[:, low:high] = local[:head_dim]
        den_ref[0, :, low:high] = local[head_dim : head_dim + 1]


def mix_kernel(
    num_ref, den_ref, pq_ref, state_ref, norm_ref, open_ref, x_ref, wout_ref, gain_ref, shift_ref, wfc_ref,
    mixed_ref, low_ref, denom_ref, resid_ref, hid_ref, act_ref, slope_ref,
):
    width = num_ref.shape[0]
    features = state_ref.shape[1]
    head_dim = features // 2
    opened = open_ref[...]
    for head in range(width // head_dim):
        low, high = (head * head_dim, (head + 1) * head_dim)
        state = parts_of(state_ref[low:high, :])
        normer = rows_of(parts_of(norm_ref[head : head + 1, :]), features)
        carry = dg(stacked(*state, normer), pq_ref[2 * low : 2 * high, :], 1, 0)
        num = num_ref[low:high, :] + opened * (carry[:head_dim] + carry[head_dim:features])
        den = den_ref[head] + opened * (carry[features : features + 1] + carry[features + 1 : features + 2])
        mixed = num / den
        denom_ref[head] = den
        mixed_ref[low:high, :] = mixed
        low_ref[low:high, :] = mixed.astype(bf16)
    resid = x_ref[...].astype(f32) + dg(low_ref[...], wout_ref[...], 0, 0)
    resid_ref[...] = resid
    unit, _ = norm_parts(resid)
    hid = (unit * gain_ref[...] + shift_ref[...]).astype(bf16)
    hid_ref[...] = hid
    hidden = wfc_ref.shape[1]
    step = hidden // 4
    root = 0.7978845608028654
    for low in range(0, hidden, step):
        pre = dg(hid, wfc_ref[:, low : low + step], 1, 0)
        square = pre * pre
        bent = jnp.tanh(root * pre * (1.0 + 0.044715 * square))
        half = 0.5 * (1.0 + bent)
        act_ref[:, low : low + step] = (pre * half).astype(bf16)
        curve = 0.5 * pre * (1.0 - bent * bent) * (root * (1.0 + 0.134145 * square))
        slope_ref[:, low : low + step] = (half + curve).astype(bf16)


def out_kernel(act_ref, slope_ref, resid_ref, cot_ref, wproj_ref, out_ref, dpre_ref):
    out_ref[...] = (resid_ref[...] + dg(act_ref[...], wproj_ref[...], 1, 0)).astype(bf16)
    hidden = act_ref.shape[1]
    step = hidden // 4
    for low in range(0, hidden, step):
        dact = dg(cot_ref[...], wproj_ref[low : low + step, :], 1, 1)
        dpre_ref[:, low : low + step] = (dact * slope_ref[:, low : low + step].astype(f32)).astype(bf16)


def back_kernel(
    dpre_ref, resid_ref, cot_ref, wfc_ref, gain_ref, wout_ref, mixed_ref, denom_ref, pq_ref, open_ref,
    dbranch_ref, dresid_ref, dnum_ref, dden_ref, state_ref, norm_ref, sums_ref,
):
    width = mixed_ref.shape[0]
    features = state_ref.shape[1]
    head_dim = features // 2
    rows = dpre_ref.shape[0]

    @pl.when(pl.program_id(0) == 0)
    def _():
        state_ref[...] = jnp.zeros_like(state_ref)
        norm_ref[...] = jnp.zeros_like(norm_ref)
        sums_ref[...] = jnp.zeros_like(sums_ref)

    dhid = dg(dpre_ref[...], wfc_ref[...], 1, 1)
    unit, scale = norm_parts(resid_ref[...])
    sums_ref[0:1, :] += jnp.sum(dhid * unit, axis=0, keepdims=True)
    sums_ref[1:2, :] += jnp.sum(dhid, axis=0, keepdims=True)
    dresid = cot_ref[...].astype(f32) + norm_back(unit, scale, gain_ref[...], dhid)
    dresid_ref[...] = dresid
    dbranch = dresid.astype(bf16)
    dbranch_ref[...] = dbranch
    dmixed_all = dg(wout_ref[...], dbranch, 1, 1)
    opened = open_ref[...]
    for head in range(width // head_dim):
        low, high = (head * head_dim, (head + 1) * head_dim)
        dmixed = dmixed_all[low:high]
        inverse = 1.0 / denom_ref[head]
        dnum = dmixed * inverse
        dden = -jnp.sum(dmixed * mixed_ref[low:high, :], axis=0, keepdims=True) * inverse
        dnum_ref[low:high, :] = dnum
        dden_ref[head] = dden
        wide = stacked(*parts_of(dnum * opened), rows_of(parts_of(dden * opened), rows))
        local = dg(wide, pq_ref[2 * low : 2 * high, :], 1, 1)
        state_ref[low:high, :] += local[:head_dim] + local[head_dim:features]
        norm_ref[head : head + 1, :] += local[features : features + 1] + local[features + 1 : features + 2]


def logit_back(phi, dphi):
    half = phi.shape[0] // 2
    up, down = (phi[:half].astype(f32), phi[half:].astype(f32))
    dup, ddown = (dphi[:half], dphi[half:])
    dup = dup - jnp.sum(dup * up, axis=0, keepdims=True)
    ddown = ddown - jnp.sum(ddown * down, axis=0, keepdims=True)
    return (up * dup - down * ddown).astype(bf16)


def local_back_kernel(
    pq_ref, pk_ref, q_ref, v_ref, dnum_ref, dden_ref, start_ref, open_ref, state_ref, norm_ref, fq_ref,
    dq_ref, gfq_ref, dphik_ref, dv_ref,
):
    tokens = pq_ref.shape[1]
    features = pq_ref.shape[0]
    step = min(256, tokens)
    state_high, state_low = parts_of(state_ref[...])
    norm_high, norm_low = parts_of(norm_ref[0])
    carried = stacked(
        state_high, state_high, state_low, rows_of((norm_high, norm_high, norm_low), features)
    )
    dphik_ref[...] = jnp.zeros_like(dphik_ref)
    dv_ref[...] = jnp.zeros_like(dv_ref)
    maps = fq_ref[...]
    gfq = jnp.zeros(gfq_ref.shape[1:], f32)
    for low in range(0, tokens, step):
        high = low + step
        start = start_ref[:, low:high]
        phi = pq_ref[:, low:high]
        num_high, num_low = parts_of(dnum_ref[:, low:high])
        dnum_low = num_high.astype(bf16)
        dden = dden_ref[0, :, low:high]
        weights = masked(dg(pk_ref[:, :high], phi, 0, 0), start, low)
        dweights = masked(dg(v_ref[:, :high], dnum_low, 0, 0) + dden, start, low)
        dv_ref[:, :high] += dg(dnum_low, weights, 1, 1)
        dphik_ref[:, :high] += dg(phi, dweights, 1, 1)
        den_high, den_low = parts_of(dden)
        arriving = stacked(num_high, num_low, num_high, rows_of((den_high, den_low, den_high), step))
        dphi = dg(pk_ref[:, :high], dweights, 1, 0)
        dphi = dphi + open_ref[:, low:high] * dg(carried, arriving, 0, 0)
        dlogit = logit_back(phi, dphi)
        gfq = gfq + dg(q_ref[:, low:high], dlogit, 1, 1)
        dq_ref[:, low:high] = dg(maps, dlogit, 1, 0).astype(bf16)
    gfq_ref[0] = gfq


def key_back_kernel(
    pk_ref, k_ref, v_ref, dphik_ref, dv_ref, tail_ref, state_ref, norm_ref, fk_ref, dkv_ref, gfk_ref
):
    features, tokens = pk_ref.shape
    head_dim = features // 2
    state_high, state_low = parts_of(state_ref[...])
    carried = stacked(state_high, state_low, rows_of(parts_of(norm_ref[0]), features))
    values = v_ref[...]
    tail = tail_ref[...]
    wide = stacked(values, values, jnp.ones((16, tokens), bf16))
    phi = pk_ref[...]
    dphi = dphik_ref[...] + tail * dg(carried, wide, 0, 0)
    both = dg(stacked(state_high, state_low), phi, 1, 0)
    dv = dv_ref[...] + tail * (both[:head_dim] + both[head_dim:])
    dlogit = logit_back(phi, dphi)
    gfk_ref[0] = dg(k_ref[...], dlogit, 1, 1)
    dkv_ref[0] = dg(fk_ref[...], dlogit, 1, 0).astype(bf16)
    dkv_ref[1] = dv.astype(bf16)


def leave_kernel(dq_ref, dkv_ref, w_ref, x_ref, gain_ref, dresid_ref, grad_ref, sums_ref):
    width = dq_ref.shape[0]

    @pl.when(pl.program_id(0) == 0)
    def _():
        sums_ref[...] = jnp.zeros_like(sums_ref)

    dhid = dg(dq_ref[...], w_ref[:, :width], 0, 1)
    dhid = dhid + dg(dkv_ref[0], w_ref[:, width : 2 * width], 0, 1)
    dhid = dhid + dg(dkv_ref[1], w_ref[:, 2 * width :], 0, 1)
    unit, scale = norm_parts(x_ref[...].astype(f32))
    sums_ref[0:1, :] += jnp.sum(dhid * unit, axis=0, keepdims=True)
    sums_ref[1:2, :] += jnp.sum(dhid, axis=0, keepdims=True)
    grad_ref[...] = dresid_ref[...] + norm_back(unit, scale, gain_ref[...], dhid)


def whole(shape):
    return pl.BlockSpec(shape, lambda i: (0,) * len(shape))


def down(rows, width):
    return pl.BlockSpec((rows, width), lambda i: (i, 0))


def across(rows, width):
    return pl.BlockSpec((rows, width), lambda i: (0, i))


def heads_across(heads, width):
    return pl.BlockSpec((heads, 1, width), lambda i: (0, 0, i))


def one_head(width):
    return pl.BlockSpec((1, 1, width), lambda i: (i, 0, 0))


def head_rows(rows, width, first=0):
    return pl.BlockSpec((rows, width), lambda i: (first + i, 0))


def shape_of(shape, dtype):
    return jax.ShapeDtypeStruct(shape, dtype)


def call(kernel, name, grid, ins, outs, shapes, args):
    return pl.pallas_call(
        kernel,
        name=name,
        grid=(grid,),
        in_specs=ins,
        out_specs=outs,
        out_shape=shapes,
        compiler_params=pltpu.CompilerParams(
            dimension_semantics=("arbitrary",), vmem_limit_bytes=grant
        ),
    )(*args)


def log2_of(count):
    return count.bit_length() - 1


def flips(grp_size, tok_size, first, second):
    pairs = []
    for place in range(grp_size * tok_size):
        grp = place // tok_size
        pairs.append((place, place ^ (second if grp % 2 else first)))
    return pairs


def carry_scan(packed, keep, backward):
    grp_size, tok_size = (lax.axis_size("grp"), lax.axis_size("tok"))
    place = lax.axis_index("grp") * tok_size + lax.axis_index("tok")
    rows = packed.shape[0]
    total = jnp.concatenate([packed, jnp.full((4, 128), keep, jnp.float32)], axis=0)
    is_keep = lax.broadcasted_iota(jnp.int32, total.shape, 0) >= rows
    prefix = jnp.where(is_keep, 1.0, 0.0)
    steps = log2_of(grp_size * tok_size)
    for step in range(steps):
        other = lax.ppermute(total, ("grp", "tok"), flips(grp_size, tok_size, 1 << step, 1 << step))
        bit = (place >> step) & 1
        later = (bit == 0) if backward else (bit == 1)
        prefix = jnp.where(later, jnp.where(is_keep, 0.0, prefix) + prefix[rows, 0] * other, prefix)
        if step + 1 < steps:
            late = jnp.where(later, total, other)
            early = jnp.where(later, other, total)
            total = jnp.where(is_keep, 0.0, late) + late[rows, 0] * early
    return prefix[:rows]


def reduce_rows(grad):
    grp_size, tok_size = (lax.axis_size("grp"), lax.axis_size("tok"))
    axes = ("grp", "tok")
    core = lax.axis_index("grp") % 2
    place = lax.axis_index("grp") * tok_size + lax.axis_index("tok")
    tok_bits, far_bits = (log2_of(tok_size), log2_of(grp_size) - 1)
    width = grad.shape[1]
    rows = grad.shape[0] // tok_size
    sub = rows // grp_size
    far = grp_size // 2
    view = grad.reshape(tok_size, 2, far * sub, width)
    mine = lax.dynamic_index_in_dim(view, core, 1, keepdims=False)
    theirs = lax.dynamic_index_in_dim(view, 1 - core, 1, keepdims=False)
    mine = mine + lax.ppermute(theirs, axes, flips(grp_size, tok_size, tok_size, tok_size))
    dims = (2,) * (tok_bits + far_bits)
    mine = mine.reshape(dims + (sub, width))
    tok_axes = list(range(tok_bits))[::-1]
    far_axes = [tok_bits + i for i in range(far_bits)][::-1]
    order_a = far_axes + tok_axes
    order_b = tok_axes + far_axes
    tail = (len(dims), len(dims) + 1)
    buf = jnp.where(
        core == 0,
        mine.transpose(*order_a, *tail),
        mine.transpose(*order_b, *tail),
    ).reshape(-1, sub, width)
    tok_flips = [1 << i for i in range(tok_bits)]
    far_flips = [(2 * tok_size) << i for i in range(far_bits)]
    flips_a = far_flips + tok_flips
    flips_b = tok_flips + far_flips
    for flip_a, flip_b in zip(flips_a, flips_b):
        bit = jnp.where(core == 0, (place & flip_a) != 0, (place & flip_b) != 0).astype(jnp.int32)
        half = buf.shape[0] // 2
        keep = lax.dynamic_slice_in_dim(buf, bit * half, half, 0)
        give = lax.dynamic_slice_in_dim(buf, (1 - bit) * half, half, 0)
        buf = keep + lax.ppermute(give, axes, flips(grp_size, tok_size, flip_a, flip_b))
    for flip in far_flips + [tok_size]:
        bit = (place & flip) != 0
        other = lax.ppermute(buf, axes, flips(grp_size, tok_size, flip, flip))
        buf = jnp.concatenate(
            [jnp.where(bit, other, buf), jnp.where(bit, buf, other)], axis=0
        )
    return buf.reshape(rows, width)


def reduce_vectors(stack):
    grp_size, tok_size = (lax.axis_size("grp"), lax.axis_size("tok"))
    count, length = stack.shape
    share = length // tok_size
    blocks = stack.reshape(count, tok_size, share).transpose(1, 0, 2)
    blocks = blocks.reshape(tok_size, count * share)
    spread = jnp.broadcast_to(blocks[None], (grp_size,) + blocks.shape)
    spread = spread.reshape(grp_size * tok_size, count * share)
    landed = lax.all_to_all(spread, ("grp", "tok"), 0, 0, tiled=True)
    return jnp.sum(landed, axis=0).reshape(count, share)


def on_device(
    layer_input,
    doc_starts,
    ln1_gain,
    ln1_shift,
    w_qkv,
    feat_q,
    feat_k,
    w_out,
    ln2_gain,
    ln2_shift,
    w_fc,
    w_proj,
    cotangent,
):
    tokens, width = layer_input.shape
    head_dim = feat_q.shape[1]
    heads = width // head_dim
    feats = 2 * head_dim
    hidden = w_fc.shape[1]
    rows = min(256, tokens)
    blocks = tokens // rows
    gain1, shift1 = (ln1_gain[None], ln1_shift[None])
    gain2, shift2 = (ln2_gain[None], ln2_shift[None])

    at = jnp.arange(tokens, dtype=jnp.int32)
    marked = (doc_starts[:, None] > 0) & (at[:, None] <= at[None, :])
    last = jnp.max(jnp.where(marked, at[:, None], -1), axis=0)
    start = jnp.maximum(last, 0)[None]
    opened = (last < 0).astype(f32)[None]
    tail = (at >= last[-1]).astype(f32)[None]
    keep = (last[-1] < 0).astype(f32)

    hid1, qkv, phi_q, phi_k, state, norm = call(
        enter_kernel, "enter", blocks,
        [down(rows, width), whole((1, width)), whole((1, width)), whole(w_qkv.shape),
         whole(feat_q.shape), whole(feat_k.shape), across(1, rows)],
        [down(rows, width), across(3 * width, rows), across(2 * width, rows), across(2 * width, rows),
         whole((width, feats)), whole((heads, feats))],
        [shape_of((tokens, width), bf16), shape_of((3 * width, tokens), bf16),
         shape_of((2 * width, tokens), bf16), shape_of((2 * width, tokens), bf16),
         shape_of((width, feats), f32), shape_of((heads, feats), f32)],
        (layer_input, gain1, shift1, w_qkv, feat_q, feat_k, tail.astype(bf16)),
    )
    carried = carry_scan(jnp.concatenate([state, norm], axis=0), keep, False)
    state_in, norm_in = (carried[:width], carried[width:])
    num, den = call(
        local_kernel, "local", heads,
        [head_rows(feats, tokens), head_rows(feats, tokens), head_rows(head_dim, tokens, 2 * heads),
         whole((1, tokens))],
        [head_rows(head_dim, tokens), one_head(tokens)],
        [shape_of((width, tokens), f32), shape_of((heads, 1, tokens), f32)],
        (phi_q, phi_k, qkv, start),
    )
    mixed, mixed_low, denom, resid, hid2, act, slope = call(
        mix_kernel, "mix", blocks,
        [across(width, rows), heads_across(heads, rows), across(2 * width, rows), whole((width, feats)),
         whole((heads, feats)), across(1, rows), down(rows, width), whole(w_out.shape),
         whole((1, width)), whole((1, width)), whole(w_fc.shape)],
        [across(width, rows), across(width, rows), heads_across(heads, rows), down(rows, width),
         down(rows, width), down(rows, hidden), down(rows, hidden)],
        [shape_of((width, tokens), f32), shape_of((width, tokens), bf16),
         shape_of((heads, 1, tokens), f32), shape_of((tokens, width), f32),
         shape_of((tokens, width), bf16), shape_of((tokens, hidden), bf16),
         shape_of((tokens, hidden), bf16)],
        (num, den, phi_q, state_in, norm_in, opened, layer_input, w_out, gain2, shift2, w_fc),
    )
    output, dpre = call(
        out_kernel, "out", blocks,
        [down(rows, hidden), down(rows, hidden), down(rows, width), down(rows, width), whole(w_proj.shape)],
        [down(rows, width), down(rows, hidden)],
        [shape_of((tokens, width), bf16), shape_of((tokens, hidden), bf16)],
        (act, slope, resid, cotangent, w_proj),
    )
    dbranch, dresid, dnum, dden, back_state, back_norm, sums2 = call(
        back_kernel, "back", blocks,
        [down(rows, hidden), down(rows, width), down(rows, width), whole(w_fc.shape), whole((1, width)),
         whole(w_out.shape), across(width, rows), heads_across(heads, rows), across(2 * width, rows),
         across(1, rows)],
        [down(rows, width), down(rows, width), across(width, rows), heads_across(heads, rows),
         whole((width, feats)), whole((heads, feats)), whole((8, width))],
        [shape_of((tokens, width), bf16), shape_of((tokens, width), f32),
         shape_of((width, tokens), f32), shape_of((heads, 1, tokens), f32),
         shape_of((width, feats), f32), shape_of((heads, feats), f32), shape_of((8, width), f32)],
        (dpre, resid, cotangent, w_fc, gain2, w_out, mixed, denom, phi_q, opened),
    )
    returned = carry_scan(jnp.concatenate([back_state, back_norm], axis=0), keep, True)
    dq, gfq, dphi_k, dv = call(
        local_back_kernel, "local_back", heads,
        [head_rows(feats, tokens), head_rows(feats, tokens), head_rows(head_dim, tokens),
         head_rows(head_dim, tokens, 2 * heads), head_rows(head_dim, tokens), one_head(tokens),
         whole((1, tokens)), whole((1, tokens)), head_rows(head_dim, feats), one_head(feats),
         head_rows(head_dim, head_dim)],
        [head_rows(head_dim, tokens), pl.BlockSpec((1, head_dim, head_dim), lambda i: (i, 0, 0)),
         head_rows(feats, tokens), head_rows(head_dim, tokens)],
        [shape_of((width, tokens), bf16), shape_of((heads, head_dim, head_dim), f32),
         shape_of((2 * width, tokens), f32), shape_of((width, tokens), f32)],
        (phi_q, phi_k, qkv, qkv, dnum, dden, start, opened, state_in, norm_in[:, None], feat_q),
    )
    dkv, gfk = call(
        key_back_kernel, "key_back", heads,
        [head_rows(feats, tokens), head_rows(head_dim, tokens, heads),
         head_rows(head_dim, tokens, 2 * heads), head_rows(feats, tokens), head_rows(head_dim, tokens),
         whole((1, tokens)), head_rows(head_dim, feats), one_head(feats), head_rows(head_dim, head_dim)],
        [pl.BlockSpec((2, head_dim, tokens), lambda i: (0, i, 0)),
         pl.BlockSpec((1, head_dim, head_dim), lambda i: (i, 0, 0))],
        [shape_of((2, width, tokens), bf16), shape_of((heads, head_dim, head_dim), f32)],
        (phi_k, qkv, qkv, dphi_k, dv, tail, returned[:width], returned[width:][:, None], feat_k),
    )
    grad_input, sums1 = call(
        leave_kernel, "leave", blocks,
        [across(width, rows), pl.BlockSpec((2, width, rows), lambda i: (0, 0, i)), whole(w_qkv.shape),
         down(rows, width), whole((1, width)), down(rows, width)],
        [down(rows, width), whole((8, width))],
        [shape_of((tokens, width), f32), shape_of((8, width), f32)],
        (dq, dkv, w_qkv, layer_input, gain1, dresid),
    )
    grad_proj = jnp.dot(act.T, cotangent, preferred_element_type=f32)
    grad_fc = jnp.dot(hid2.T, dpre, preferred_element_type=f32)
    grad_out = jnp.dot(mixed_low, dbranch, preferred_element_type=f32)
    dqkv = jnp.concatenate([dq[None], dkv], axis=0).reshape(3 * width, tokens)
    grad_qkv = jnp.einsum("td,ct->dc", hid1, dqkv, preferred_element_type=f32)
    vectors = reduce_vectors(jnp.concatenate([sums1[:2], sums2[:2]], axis=0))
    share_feat = reduce_rows(
        jnp.concatenate([gfq.reshape(width, head_dim), gfk.reshape(width, head_dim)], axis=1)
    )
    return (
        output,
        grad_input,
        vectors[0],
        vectors[1],
        reduce_rows(grad_qkv),
        share_feat[:, :head_dim],
        share_feat[:, head_dim:],
        reduce_rows(grad_out),
        vectors[2],
        vectors[3],
        reduce_rows(grad_fc),
        reduce_rows(grad_proj),
    )


def solution(mesh):
    in_specs = (
        P(("grp", "tok"), None),
        P(("grp", "tok")),
        P(),
        P(),
        P(),
        P(),
        P(),
        P(),
        P(),
        P(),
        P(),
        P(),
        P(("grp", "tok"), None),
    )
    out_specs = (
        P(("grp", "tok"), None),
        P(("grp", "tok"), None),
        P("tok"),
        P("tok"),
        P("tok", None),
        P("tok", None),
        P("tok", None),
        P("tok", None),
        P("tok"),
        P("tok"),
        P("tok", None),
        P("tok", None),
    )
    return jax.shard_map(
        on_device, mesh=mesh, in_specs=in_specs, out_specs=out_specs, check_vma=False
    )
```

```python
from functools import partial

import jax
import jax.numpy as jnp
from jax import lax
from jax.experimental import pallas as pl
from jax.experimental.pallas import tpu as pltpu
from jax.sharding import PartitionSpec as P


eps = 1e-05
f32 = jnp.float32
bf16 = jnp.bfloat16
grant = 56 * 1024 * 1024


def dg(left, right, left_dim, right_dim):
    dims = (((left_dim,), (right_dim,)), ((), ()))
    return lax.dot_general(left, right, dims, preferred_element_type=f32)


def parts_of(value):
    high = value.astype(bf16).astype(f32)
    return high, value - high


def rows_of(rows, width):
    at = lax.broadcasted_iota(jnp.int32, (16, width), 0)
    block = jnp.zeros((16, width), f32)
    for place, row in enumerate(rows):
        block = jnp.where(at == place, row, block)
    return block


def stacked(*blocks):
    return jnp.concatenate([block.astype(bf16) for block in blocks], axis=0)


def norm_parts(value):
    centered = value - jnp.mean(value, axis=1, keepdims=True)
    variance = jnp.mean(centered * centered, axis=1, keepdims=True)
    scale = lax.rsqrt(variance + eps)
    return centered * scale, scale


def norm_back(unit, scale, gain, grad):
    scaled = grad * gain
    along = jnp.mean(scaled * unit, axis=1, keepdims=True)
    return scale * (scaled - jnp.mean(scaled, axis=1, keepdims=True) - unit * along)


def enter_kernel(
    x_ref, gain_ref, shift_ref, w_ref, fq_ref, fk_ref, tail_ref,
    hid_ref, qkv_ref, pq_ref, pk_ref, state_ref, norm_ref,
):
    width, head_dim = fq_ref.shape
    rows = x_ref.shape[0]
    unit, _ = norm_parts(x_ref[...].astype(f32))
    hid = (unit * gain_ref[...] + shift_ref[...]).astype(bf16)
    hid_ref[...] = hid
    qkv_ref[...] = dg(w_ref[...], hid, 0, 1).astype(bf16)

    @pl.when(pl.program_id(0) == 0)
    def _():
        state_ref[...] = jnp.zeros_like(state_ref)
        norm_ref[...] = jnp.zeros_like(norm_ref)

    def features(maps, token_rows):
        logits = dg(maps, token_rows, 0, 0)
        up = jnp.exp(logits - jnp.max(logits, axis=0, keepdims=True))
        down = jnp.exp(jnp.min(logits, axis=0, keepdims=True) - logits)
        up = up / jnp.sum(up, axis=0, keepdims=True)
        down = down / jnp.sum(down, axis=0, keepdims=True)
        return stacked(up, down)

    ones = jnp.ones((16, rows), bf16)
    for head in range(width // head_dim):
        low, high = (head * head_dim, (head + 1) * head_dim)
        pq_ref[2 * low : 2 * high, :] = features(fq_ref[low:high, :], qkv_ref[low:high, :])
        phi = features(fk_ref[low:high, :], qkv_ref[width + low : width + high, :])
        pk_ref[2 * low : 2 * high, :] = phi
        wide = stacked(qkv_ref[2 * width + low : 2 * width + high, :], ones)
        local = dg(wide, phi * tail_ref[...], 1, 1)
        state_ref[low:high, :] += local[:head_dim]
        norm_ref[head : head + 1, :] += local[head_dim : head_dim + 1]


def masked(scores, start, offset):
    key_at = lax.broadcasted_iota(jnp.int32, scores.shape, 0)
    query_at = lax.broadcasted_iota(jnp.int32, scores.shape, 1) + offset
    allowed = (key_at >= start) & (key_at <= query_at)
    return jnp.where(allowed, scores, 0.0).astype(bf16)


def local_kernel(pq_ref, pk_ref, v_ref, start_ref, num_ref, den_ref):
    tokens = pq_ref.shape[1]
    head_dim = v_ref.shape[0]
    step = min(256, tokens)
    for low in range(0, tokens, step):
        high = low + step
        scores = dg(pk_ref[:, :high], pq_ref[:, low:high], 0, 0)
        weights = masked(scores, start_ref[:, low:high], low)
        wide = stacked(v_ref[:, :high], jnp.ones((16, high), bf16))
        local = dg(wide, weights, 1, 0)
        num_ref[:, low:high] = local[:head_dim]
        den_ref[0, :, low:high] = local[head_dim : head_dim + 1]


def mix_kernel(
    num0_ref, num1_ref, den0_ref, den1_ref, pq_ref, state_ref, norm_ref, open_ref, x_ref, wout_ref, gain_ref, shift_ref, wfc_ref,
    mixed_ref, low_ref, denom_ref, resid_ref, hid_ref, act_ref, slope_ref,
):
    width, features = state_ref.shape
    head_dim = features // 2
    opened = open_ref[...]
    for head in range(width // head_dim):
        low, high = (head * head_dim, (head + 1) * head_dim)
        state = parts_of(state_ref[low:high, :])
        normer = rows_of(parts_of(norm_ref[head : head + 1, :]), features)
        carry = dg(stacked(*state, normer), pq_ref[2 * low : 2 * high, :], 1, 0)
        half = width // 2
        num_ref, den_ref = (num0_ref, den0_ref) if low < half else (num1_ref, den1_ref)
        num = num_ref[low % half : low % half + head_dim, :]
        num = num + opened * (carry[:head_dim] + carry[head_dim:features])
        den = den_ref[head % (half // head_dim)] + opened * (carry[features : features + 1] + carry[features + 1 : features + 2])
        mixed = num / den
        denom_ref[head] = den
        mixed_ref[low:high, :] = mixed
        low_ref[low:high, :] = mixed.astype(bf16)
    resid = x_ref[...].astype(f32) + dg(low_ref[...], wout_ref[...], 0, 0)
    resid_ref[...] = resid
    unit, _ = norm_parts(resid)
    hid = (unit * gain_ref[...] + shift_ref[...]).astype(bf16)
    hid_ref[...] = hid
    hidden = wfc_ref.shape[1]
    step = hidden // 4
    root = 0.7978845608028654
    for low in range(0, hidden, step):
        pre = dg(hid, wfc_ref[:, low : low + step], 1, 0)
        square = pre * pre
        bent = jnp.tanh(root * pre * (1.0 + 0.044715 * square))
        half = 0.5 * (1.0 + bent)
        act_ref[:, low : low + step] = (pre * half).astype(bf16)
        curve = 0.5 * pre * (1.0 - bent * bent) * (root * (1.0 + 0.134145 * square))
        slope_ref[:, low : low + step] = (half + curve).astype(bf16)


def slope_kernel(slope_ref, cot_ref, wproj_ref, dpre_ref):
    hidden = slope_ref.shape[1]
    step = hidden // 4
    for low in range(0, hidden, step):
        dact = dg(cot_ref[...], wproj_ref[low : low + step, :], 1, 1)
        dpre_ref[:, low : low + step] = (dact * slope_ref[:, low : low + step].astype(f32)).astype(bf16)


def out_kernel(act_ref, resid_ref, wproj_ref, out_ref):
    out_ref[...] = (resid_ref[...] + dg(act_ref[...], wproj_ref[...], 1, 0)).astype(bf16)


def back_kernel(
    dpre_ref, resid_ref, cot_ref, wfc_ref, gain_ref, wout_ref, mixed_ref, denom_ref, pq_ref, open_ref,
    dbranch_ref, dresid_ref, dnum_ref, dden_ref, state_ref, norm_ref, sums_ref,
):
    width = mixed_ref.shape[0]
    features = state_ref.shape[1]
    head_dim = features // 2
    rows = dpre_ref.shape[0]

    @pl.when(pl.program_id(0) == 0)
    def _():
        state_ref[...] = jnp.zeros_like(state_ref)
        norm_ref[...] = jnp.zeros_like(norm_ref)
        sums_ref[...] = jnp.zeros_like(sums_ref)

    dhid = dg(dpre_ref[...], wfc_ref[...], 1, 1)
    unit, scale = norm_parts(resid_ref[...])
    sums_ref[0:1, :] += jnp.sum(dhid * unit, axis=0, keepdims=True)
    sums_ref[1:2, :] += jnp.sum(dhid, axis=0, keepdims=True)
    dresid = cot_ref[...].astype(f32) + norm_back(unit, scale, gain_ref[...], dhid)
    dresid_ref[...] = dresid
    dbranch = dresid.astype(bf16)
    dbranch_ref[...] = dbranch
    dmixed_all = dg(wout_ref[...], dbranch, 1, 1)
    opened = open_ref[...]
    for head in range(width // head_dim):
        low, high = (head * head_dim, (head + 1) * head_dim)
        dmixed = dmixed_all[low:high]
        inverse = 1.0 / denom_ref[head]
        dnum = dmixed * inverse
        dden = -jnp.sum(dmixed * mixed_ref[low:high, :], axis=0, keepdims=True) * inverse
        dnum_ref[low:high, :] = dnum
        dden_ref[head] = dden
        wide = stacked(*parts_of(dnum * opened), rows_of(parts_of(dden * opened), rows))
        local = dg(wide, pq_ref[2 * low : 2 * high, :], 1, 1)
        state_ref[low:high, :] += local[:head_dim] + local[head_dim:features]
        norm_ref[head : head + 1, :] += local[features : features + 1] + local[features + 1 : features + 2]


def logit_back(phi, dphi):
    half = phi.shape[0] // 2
    up, down = (phi[:half].astype(f32), phi[half:].astype(f32))
    dup, ddown = (dphi[:half], dphi[half:])
    dup = dup - jnp.sum(dup * up, axis=0, keepdims=True)
    ddown = ddown - jnp.sum(ddown * down, axis=0, keepdims=True)
    return (up * dup - down * ddown).astype(bf16)


def local_back_kernel(
    pq_ref, pk_ref, q_ref, v_ref, dnum_ref, dden_ref, start_ref, open_ref, state_ref, norm_ref, fq_ref,
    dq_ref, gfq_ref, dphik_ref, dv_ref,
):
    tokens = pq_ref.shape[1]
    features = pq_ref.shape[0]
    step = min(256, tokens)
    state_high, state_low = parts_of(state_ref[...])
    norm_high, norm_low = parts_of(norm_ref[0])
    carried = stacked(
        state_high, state_high, state_low, rows_of((norm_high, norm_high, norm_low), features)
    )
    dphik_ref[...] = jnp.zeros_like(dphik_ref)
    dv_ref[...] = jnp.zeros_like(dv_ref)
    maps = fq_ref[...]
    gfq = jnp.zeros(gfq_ref.shape[1:], f32)
    for low in range(0, tokens, step):
        high = low + step
        start = start_ref[:, low:high]
        phi = pq_ref[:, low:high]
        num_high, num_low = parts_of(dnum_ref[:, low:high])
        dnum_low = num_high.astype(bf16)
        dden = dden_ref[0, :, low:high]
        weights = masked(dg(pk_ref[:, :high], phi, 0, 0), start, low)
        dweights = masked(dg(v_ref[:, :high], dnum_low, 0, 0) + dden, start, low)
        dv_ref[:, :high] += dg(dnum_low, weights, 1, 1)
        dphik_ref[:, :high] += dg(phi, dweights, 1, 1)
        den_high, den_low = parts_of(dden)
        arriving = stacked(num_high, num_low, num_high, rows_of((den_high, den_low, den_high), step))
        dphi = dg(pk_ref[:, :high], dweights, 1, 0)
        dphi = dphi + open_ref[:, low:high] * dg(carried, arriving, 0, 0)
        dlogit = logit_back(phi, dphi)
        gfq = gfq + dg(q_ref[:, low:high], dlogit, 1, 1)
        dq_ref[:, low:high] = dg(maps, dlogit, 1, 0).astype(bf16)
    gfq_ref[0] = gfq


def key_back_kernel(
    pk_ref, k_ref, v_ref, dphik0_ref, dphik1_ref, dv0_ref, dv1_ref, tail_ref, state_ref, norm_ref, fk_ref,
    dkv_ref, gfk_ref,
):
    features, tokens = pk_ref.shape
    head_dim = features // 2
    state_high, state_low = parts_of(state_ref[...])
    carried = stacked(state_high, state_low, rows_of(parts_of(norm_ref[0]), features))
    values = v_ref[...]
    tail = tail_ref[...]
    wide = stacked(values, values, jnp.ones((16, tokens), bf16))
    phi = pk_ref[...]
    early = pl.program_id(0) < pl.num_programs(0) // 2
    dphi = jnp.where(early, dphik0_ref[...], dphik1_ref[...]) + tail * dg(carried, wide, 0, 0)
    both = dg(stacked(state_high, state_low), phi, 1, 0)
    dv = jnp.where(early, dv0_ref[...], dv1_ref[...]) + tail * (both[:head_dim] + both[head_dim:])
    dlogit = logit_back(phi, dphi)
    gfk_ref[0] = dg(k_ref[...], dlogit, 1, 1)
    dkv_ref[0] = dg(fk_ref[...], dlogit, 1, 0).astype(bf16)
    dkv_ref[1] = dv.astype(bf16)


def leave_kernel(dq0_ref, dq1_ref, dkv_ref, w_ref, x_ref, gain_ref, dresid_ref, grad_ref, sums_ref):
    width = x_ref.shape[1]

    @pl.when(pl.program_id(0) == 0)
    def _():
        sums_ref[...] = jnp.zeros_like(sums_ref)

    dq = jnp.concatenate([dq0_ref[...], dq1_ref[...]], axis=0)
    dhid = dg(dq, w_ref[:, :width], 0, 1)
    dhid = dhid + dg(dkv_ref[0], w_ref[:, width : 2 * width], 0, 1)
    dhid = dhid + dg(dkv_ref[1], w_ref[:, 2 * width :], 0, 1)
    unit, scale = norm_parts(x_ref[...].astype(f32))
    sums_ref[0:1, :] += jnp.sum(dhid * unit, axis=0, keepdims=True)
    sums_ref[1:2, :] += jnp.sum(dhid, axis=0, keepdims=True)
    grad_ref[...] = dresid_ref[...] + norm_back(unit, scale, gain_ref[...], dhid)


def whole(shape):
    return pl.BlockSpec(shape, lambda i: (0,) * len(shape))


def down(rows, width):
    return pl.BlockSpec((rows, width), lambda i: (i, 0))


def across(rows, width):
    return pl.BlockSpec((rows, width), lambda i: (0, i))


def heads_across(heads, width):
    return pl.BlockSpec((heads, 1, width), lambda i: (0, 0, i))


def one_head(width, first=0):
    return pl.BlockSpec((1, 1, width), lambda i: (first + i, 0, 0))


def head_rows(rows, width, first=0):
    return pl.BlockSpec((rows, width), lambda i: (first + i, 0))


def shape_of(shape, dtype):
    return jax.ShapeDtypeStruct(shape, dtype)


def call(kernel, grid, ins, outs, shapes, args):
    return pl.pallas_call(
        kernel,
        grid=(grid,),
        in_specs=ins,
        out_specs=outs,
        out_shape=shapes,
        compiler_params=pltpu.CompilerParams(
            dimension_semantics=("arbitrary",), vmem_limit_bytes=grant
        ),
    )(*args)


def log2_of(count):
    return count.bit_length() - 1


def sizes():
    return (lax.axis_size("grp"), lax.axis_size("tok"))


def place_of():
    return lax.axis_index("grp") * lax.axis_size("tok") + lax.axis_index("tok")


def flips(first, second):
    grp_size, tok_size = sizes()
    pairs = []
    for place in range(grp_size * tok_size):
        pairs.append((place, place ^ (second if (place // tok_size) % 2 else first)))
    return pairs


def far_flips():
    grp_size, tok_size = sizes()
    return [(2 * tok_size) << bit for bit in range(log2_of(grp_size) - 1)]


def order_of(turn):
    tok_bits = [1 << bit for bit in range(log2_of(lax.axis_size("tok")))]
    near = far_flips() + tok_bits[:-1]
    turn = turn % len(near)
    return near[turn:] + near[:turn] + tok_bits[-1:]


def slots_of(turn):
    grp_size, tok_size = sizes()
    order = order_of(turn)
    slots = []
    for tok in range(tok_size):
        for far in range(grp_size // 2):
            place = far * 2 * tok_size + tok
            bits = [(place // flip) % 2 for flip in order]
            slots.append(sum(bit << (len(bits) - 1 - at) for at, bit in enumerate(bits)))
    return jnp.array(slots, jnp.int32)


def tables_of(turns):
    core = lax.axis_index("grp") % 2
    own = lax.axis_index("tok") * (lax.axis_size("grp") // 2) + lax.axis_index("grp") // 2
    even, odd = (slots_of(turns[0]), slots_of(turns[1]))
    mine = jnp.where(core == 0, even, odd)
    theirs = jnp.where(core == 0, odd, even)
    mine = jnp.concatenate([mine ^ mine[own], core[None].astype(jnp.int32)])
    theirs = jnp.concatenate([theirs ^ theirs[own], (1 - core)[None].astype(jnp.int32)])
    return mine, theirs


def product_kernel(forms, has_tail, has_other, table_ref, *refs):
    count = len(forms)
    ins, refs = (refs[: 2 * count], refs[2 * count :])
    tail_ref, refs = (refs[0], refs[1:]) if has_tail else (None, refs)
    other_ref, refs = (refs[0], refs[1:]) if has_other else (None, refs)
    pieces = table_ref.shape[0] - 1
    piece_rows = refs[0].shape[1]
    at = 0
    blocks = []
    for place, (left_dim, right_dim) in enumerate(forms):
        left, right = (ins[2 * place][...], ins[2 * place + 1][...])
        right = right.reshape(right.shape[-2:])
        value = dg(left, right, left_dim, right_dim)
        blocks.append((at, value))
        at += value.shape[1]
    if has_tail:
        blocks.append((at, tail_ref[0]))
    rows = blocks[0][1].shape[0]
    here = rows // piece_rows
    base = pl.program_id(0) * here
    for piece in range(here):
        slot = table_ref[base + piece]
        span = slice(piece * piece_rows, (piece + 1) * piece_rows)
        for column, value in blocks:
            cut = value[span]
            lanes = slice(column, column + cut.shape[1])
            if not has_other:
                refs[0][slot, :, lanes] = cut
                continue
            cut = cut + other_ref[slot, :, lanes]
            keep_ref, give_ref = refs
            half = pieces // 2

            @pl.when(slot < half)
            def _(cut=cut, lanes=lanes):
                keep_ref[slot, :, lanes] = cut

            @pl.when(slot >= half)
            def _(cut=cut, lanes=lanes):
                give_ref[slot - half, :, lanes] = cut


def products(table, forms, ins, specs, rows, block_rows, columns, tail=None, other=None):
    pieces = table.shape[0] - 1
    piece_rows = rows // pieces
    shape = (pieces, piece_rows, columns)
    whole_spec = lambda dims: pl.BlockSpec(dims, lambda i, t: (0,) * len(dims))
    specs = list(specs)
    ins = list(ins)
    if tail is not None:
        ins.append(tail)
        specs.append(pl.BlockSpec((1, block_rows, tail.shape[2]), lambda i, t: (t[pieces], i, 0)))
    if other is not None:
        ins.append(other)
        specs.append(whole_spec(shape))
        half = (pieces // 2, piece_rows, columns)
        outs = [whole_spec(half), whole_spec(half)]
        shapes = [shape_of(half, f32), shape_of(half, f32)]
    else:
        outs = whole_spec(shape)
        shapes = shape_of(shape, f32)
    return pl.pallas_call(
        partial(product_kernel, forms, tail is not None, other is not None),
        grid_spec=pltpu.PrefetchScalarGridSpec(
            num_scalar_prefetch=1, grid=(rows // block_rows,), in_specs=specs, out_specs=outs
        ),
        out_shape=shapes,
        compiler_params=pltpu.CompilerParams(
            dimension_semantics=("arbitrary",), vmem_limit_bytes=grant
        ),
    )(table, *ins)


def send(value, first, second):
    return lax.ppermute(value, ("grp", "tok"), flips(first, second))


def swap_cores(value):
    tok_size = lax.axis_size("tok")
    return send(value, tok_size, tok_size)


def fold(keep, give, turns):
    orders = (order_of(turns[0]), order_of(turns[1]))
    for even, odd in zip(*orders):
        other = send(give, even, odd)
        half = keep.shape[0] // 2
        if half:
            give = keep[half:] + other[half:]
            keep = keep[:half] + other[:half]
        else:
            keep = keep + other
    for flip in far_flips():
        bit = (place_of() & flip) != 0
        other = send(keep, flip, flip)
        keep = jnp.concatenate(
            [jnp.where(bit, other, keep), jnp.where(bit, keep, other)], axis=0
        )
    keep = keep.reshape(-1, keep.shape[2])
    other = swap_cores(keep)
    core = lax.axis_index("grp") % 2
    return (jnp.where(core == 0, keep, other), jnp.where(core == 0, other, keep))


def chain_kernel(backward, got_ref, out_ref):
    count, rows, lanes = got_ref.shape

    def step(at, so_far):
        block = count - 1 - at if backward else at
        out_ref[block] = so_far
        local = got_ref[block]
        return local + local[rows - 1 :, lanes - 1 :] * so_far

    lax.fori_loop(0, count, step, jnp.zeros((rows, lanes), f32))


def carry_scan(state, norm, keep, backward):
    grp_size, tok_size = sizes()
    count = grp_size * tok_size
    lanes = state.shape[1]
    share = state.shape[0] // count
    spare = norm.size // count
    extra = jnp.concatenate(
        [norm.reshape(count, spare), jnp.zeros((count, lanes - 1 - spare), f32), jnp.full((count, 1), keep)],
        axis=1,
    )
    packed = jnp.concatenate([state.reshape(count, share, lanes), extra[:, None]], axis=1)
    landed = lax.all_to_all(packed, ("grp", "tok"), 0, 0, tiled=True)
    summed = pl.pallas_call(
        partial(chain_kernel, backward),
        out_shape=shape_of(landed.shape, f32),
        compiler_params=pltpu.CompilerParams(vmem_limit_bytes=grant),
    )(landed)
    home = lax.all_to_all(summed, ("grp", "tok"), 0, 0, tiled=True)
    return home[:, :share].reshape(state.shape), home[:, share, :spare].reshape(norm.shape)


def reduce_vectors(stack):
    grp_size, tok_size = sizes()
    count, length = stack.shape
    share = length // tok_size
    blocks = stack.reshape(count, tok_size, share).transpose(1, 0, 2)
    blocks = blocks.reshape(tok_size, count * share)
    spread = jnp.broadcast_to(blocks[None], (grp_size,) + blocks.shape)
    spread = spread.reshape(grp_size * tok_size, count * share)
    landed = lax.all_to_all(spread, ("grp", "tok"), 0, 0, tiled=True)
    return jnp.sum(landed, axis=0).reshape(count, share)


def on_device(
    layer_input,
    doc_starts,
    ln1_gain,
    ln1_shift,
    w_qkv,
    feat_q,
    feat_k,
    w_out,
    ln2_gain,
    ln2_shift,
    w_fc,
    w_proj,
    cotangent,
):
    tokens, width = layer_input.shape
    head_dim = feat_q.shape[1]
    heads = width // head_dim
    feats = 2 * head_dim
    hidden = w_fc.shape[1]
    rows = min(256, tokens)
    blocks = tokens // rows
    gain1, shift1 = (ln1_gain[None], ln1_shift[None])
    gain2, shift2 = (ln2_gain[None], ln2_shift[None])

    at = jnp.arange(tokens, dtype=jnp.int32)
    marked = (doc_starts[:, None] > 0) & (at[:, None] <= at[None, :])
    last = jnp.max(jnp.where(marked, at[:, None], -1), axis=0)
    start = jnp.maximum(last, 0)[None]
    opened = (last < 0).astype(f32)[None]
    tail = (at >= last[-1]).astype(f32)[None]
    keep = (last[-1] < 0).astype(f32)

    hid1, qkv, phi_q, phi_k, state, norm = call(
        enter_kernel, blocks,
        [down(rows, width), whole((1, width)), whole((1, width)), whole(w_qkv.shape),
         whole(feat_q.shape), whole(feat_k.shape), across(1, rows)],
        [down(rows, width), across(3 * width, rows), across(2 * width, rows), across(2 * width, rows),
         whole((width, feats)), whole((heads, feats))],
        [shape_of((tokens, width), bf16), shape_of((3 * width, tokens), bf16),
         shape_of((2 * width, tokens), bf16), shape_of((2 * width, tokens), bf16),
         shape_of((width, feats), f32), shape_of((heads, feats), f32)],
        (layer_input, gain1, shift1, w_qkv, feat_q, feat_k, tail.astype(bf16)),
    )
    state_in, norm_in = carry_scan(state, norm, keep, False)
    part = heads // 2
    locals_ = [
        call(
            local_kernel, part,
            [head_rows(feats, tokens, at * part), head_rows(feats, tokens, at * part),
             head_rows(head_dim, tokens, 2 * heads + at * part), whole((1, tokens))],
            [head_rows(head_dim, tokens), one_head(tokens)],
            [shape_of((width // 2, tokens), f32), shape_of((part, 1, tokens), f32)],
            (phi_q, phi_k, qkv, start),
        )
        for at in range(2)
    ]
    mixed, mixed_low, denom, resid, hid2, act, slope = call(
        mix_kernel, blocks,
        [across(width // 2, rows), across(width // 2, rows), heads_across(part, rows),
         heads_across(part, rows), across(2 * width, rows), whole((width, feats)),
         whole((heads, feats)), across(1, rows), down(rows, width), whole(w_out.shape),
         whole((1, width)), whole((1, width)), whole(w_fc.shape)],
        [across(width, rows), across(width, rows), heads_across(heads, rows), down(rows, width),
         down(rows, width), down(rows, hidden), down(rows, hidden)],
        [shape_of((width, tokens), f32), shape_of((width, tokens), bf16),
         shape_of((heads, 1, tokens), f32), shape_of((tokens, width), f32),
         shape_of((tokens, width), bf16), shape_of((tokens, hidden), bf16),
         shape_of((tokens, hidden), bf16)],
        (locals_[0][0], locals_[1][0], locals_[0][1], locals_[1][1], phi_q, state_in, norm_in, opened, layer_input, w_out, gain2, shift2, w_fc),
    )
    half = width // 2
    pair = lambda rows, columns: pl.BlockSpec((rows, columns), lambda i, t: (0, i))
    mine_a, theirs_a = tables_of((0, 1))
    mine_b, theirs_b = tables_of((2, 0))
    mine_c, theirs_c = tables_of((1, 2))
    mine_d, theirs_d = tables_of((0, 1))
    last_at = mine_a.shape[0] - 1
    right_half = lambda columns: pl.BlockSpec((tokens, columns), lambda i, t: (0, t[last_at]))
    plain = lambda rows_: pl.BlockSpec((rows_, tokens), lambda i, t: (0, 0))
    chosen = lambda which: pl.BlockSpec((1, half, tokens), lambda i, t: (which, t[last_at], 0))

    def group_a(table, other=None):
        return products(
            table, ((0, 0),), (act, cotangent), (pair(tokens, half), right_half(half)),
            hidden, half, half, None, other,
        )

    other_a = swap_cores(group_a(theirs_a))
    (dpre,) = call(
        slope_kernel, blocks,
        [down(rows, hidden), down(rows, width), whole(w_proj.shape)],
        [down(rows, hidden)],
        [shape_of((tokens, hidden), bf16)],
        (slope, cotangent, w_proj),
    )
    keep_a, give_a = group_a(mine_a, other_a)

    def group_b(table, other=None):
        return products(
            table, ((0, 0),), (hid2, dpre), (pair(tokens, half), right_half(hidden // 2)),
            width, half, hidden // 2, None, other,
        )

    other_b = swap_cores(group_b(theirs_b))
    (output,) = call(
        out_kernel, blocks,
        [down(rows, hidden), down(rows, width), whole(w_proj.shape)],
        [down(rows, width)],
        [shape_of((tokens, width), bf16)],
        (act, resid, w_proj),
    )
    keep_b, give_b = group_b(mine_b, other_b)
    dbranch, dresid, dnum, dden, back_state, back_norm, sums2 = call(
        back_kernel, blocks,
        [down(rows, hidden), down(rows, width), down(rows, width), whole(w_fc.shape), whole((1, width)),
         whole(w_out.shape), across(width, rows), heads_across(heads, rows), across(2 * width, rows),
         across(1, rows)],
        [down(rows, width), down(rows, width), across(width, rows), heads_across(heads, rows),
         whole((width, feats)), whole((heads, feats)), whole((8, width))],
        [shape_of((tokens, width), bf16), shape_of((tokens, width), f32),
         shape_of((width, tokens), f32), shape_of((heads, 1, tokens), f32),
         shape_of((width, feats), f32), shape_of((heads, feats), f32), shape_of((8, width), f32)],
        (dpre, resid, cotangent, w_fc, gain2, w_out, mixed, denom, phi_q, opened),
    )
    state_back, norm_back_in = carry_scan(back_state, back_norm, keep, True)
    split = [
        call(
            local_back_kernel, part,
            [head_rows(feats, tokens, at * part), head_rows(feats, tokens, at * part),
             head_rows(head_dim, tokens, at * part), head_rows(head_dim, tokens, 2 * heads + at * part),
             head_rows(head_dim, tokens, at * part), one_head(tokens, at * part),
             whole((1, tokens)), whole((1, tokens)), head_rows(head_dim, feats, at * part),
             one_head(feats, at * part), head_rows(head_dim, head_dim, at * part)],
            [head_rows(head_dim, tokens), pl.BlockSpec((1, head_dim, head_dim), lambda i: (i, 0, 0)),
             head_rows(feats, tokens), head_rows(head_dim, tokens)],
            [shape_of((width // 2, tokens), bf16), shape_of((part, head_dim, head_dim), f32),
             shape_of((width, tokens), f32), shape_of((width // 2, tokens), f32)],
            (phi_q, phi_k, qkv, qkv, dnum, dden, start, opened, state_in, norm_in[:, None], feat_q),
        )
        for at in range(2)
    ]
    gfq = jnp.concatenate([split[0][1], split[1][1]], axis=0)
    lower = lambda rows_: pl.BlockSpec((rows_, tokens), lambda i: (jnp.minimum(i, part - 1), 0))
    upper = lambda rows_: pl.BlockSpec((rows_, tokens), lambda i: (jnp.maximum(i - part, 0), 0))
    dkv, gfk = call(
        key_back_kernel, heads,
        [head_rows(feats, tokens), head_rows(head_dim, tokens, heads),
         head_rows(head_dim, tokens, 2 * heads), lower(feats), upper(feats), lower(head_dim), upper(head_dim),
         whole((1, tokens)), head_rows(head_dim, feats), one_head(feats), head_rows(head_dim, head_dim)],
        [pl.BlockSpec((2, head_dim, tokens), lambda i: (0, i, 0)),
         pl.BlockSpec((1, head_dim, head_dim), lambda i: (i, 0, 0))],
        [shape_of((2, width, tokens), bf16), shape_of((heads, head_dim, head_dim), f32)],
        (phi_k, qkv, qkv, split[0][2], split[1][2], split[0][3], split[1][3], tail, state_back, norm_back_in[:, None], feat_k),
    )
    grad_input, sums1 = call(
        leave_kernel, blocks,
        [across(width // 2, rows), across(width // 2, rows),
         pl.BlockSpec((2, width, rows), lambda i: (0, 0, i)), whole(w_qkv.shape),
         down(rows, width), whole((1, width)), down(rows, width)],
        [down(rows, width), whole((8, width))],
        [shape_of((tokens, width), f32), shape_of((8, width), f32)],
        (split[0][0], split[1][0], dkv, w_qkv, layer_input, gain1, dresid),
    )

    first_core = lax.axis_index("grp") % 2 == 0

    def group_c(table, flip, other=None):
        chosen_q = jnp.where(first_core != flip, split[0][0], split[1][0])
        return products(
            table, ((1, 0), (0, 1)), (mixed_low, dbranch, hid1, chosen_q),
            (pl.BlockSpec((half, tokens), lambda i, t: (i, 0)), right_half(half), pair(tokens, half),
             plain(half)),
            width, half, 2 * half, None, other,
        )

    other_c = swap_cores(group_c(theirs_c, True))
    keep_c, give_c = group_c(mine_c, False, other_c)
    feats_both = jnp.stack([gfq.reshape(width, head_dim), gfk.reshape(width, head_dim)])
    feats_both = jnp.pad(feats_both, ((0, 0), (0, 0), (0, feats - head_dim)))

    def group_d(table, other=None):
        return products(
            table, ((0, 1), (0, 1)), (hid1, dkv, hid1, dkv),
            (pair(tokens, half), chosen(0), pair(tokens, half), chosen(1)),
            width, half, 2 * half + feats, feats_both, other,
        )

    other_d = swap_cores(group_d(theirs_d))
    keep_d, give_d = group_d(mine_d, other_d)
    vectors = reduce_vectors(jnp.concatenate([sums1[:2], sums2[:2]], axis=0))
    grad_proj = jnp.concatenate(fold(keep_a, give_a, (0, 1)), axis=1)
    grad_fc = jnp.concatenate(fold(keep_b, give_b, (2, 0)), axis=1)
    c_pair = fold(keep_c, give_c, (1, 2))
    d_pair = fold(keep_d, give_d, (0, 1))
    grad_out = jnp.concatenate([part[:, :half] for part in c_pair], axis=1)
    grad_qkv = jnp.concatenate(
        [part[:, half:] for part in c_pair]
        + [part[:, :half] for part in d_pair]
        + [part[:, half : 2 * half] for part in d_pair],
        axis=1,
    )
    return (
        output,
        grad_input,
        vectors[0],
        vectors[1],
        grad_qkv,
        d_pair[0][:, 2 * half : 2 * half + head_dim],
        d_pair[1][:, 2 * half : 2 * half + head_dim],
        grad_out,
        vectors[2],
        vectors[3],
        grad_fc,
        grad_proj,
    )


def solution(mesh):
    in_specs = (
        P(("grp", "tok"), None),
        P(("grp", "tok")),
        P(),
        P(),
        P(),
        P(),
        P(),
        P(),
        P(),
        P(),
        P(),
        P(),
        P(("grp", "tok"), None),
    )
    out_specs = (
        P(("grp", "tok"), None),
        P(("grp", "tok"), None),
        P("tok"),
        P("tok"),
        P("tok", None),
        P("tok", None),
        P("tok", None),
        P("tok", None),
        P("tok"),
        P("tok"),
        P("tok", None),
        P("tok", None),
    )

    return jax.shard_map(on_device, mesh=mesh, in_specs=in_specs, out_specs=out_specs, check_vma=False)
```

```python
from functools import partial

import jax
import jax.numpy as jnp
from jax import lax
from jax.experimental import pallas as pl
from jax.experimental.pallas import tpu as pltpu
from jax.sharding import PartitionSpec as P


eps = 1e-05
f32 = jnp.float32
bf16 = jnp.bfloat16
grant = 58 * 1024 * 1024


def dg(left, right, left_dim, right_dim):
    dims = (((left_dim,), (right_dim,)), ((), ()))
    return lax.dot_general(left, right, dims, preferred_element_type=f32)


def parts_of(value):
    high = value.astype(bf16).astype(f32)
    return high, value - high


def rows_of(rows, width):
    at = lax.broadcasted_iota(jnp.int32, (16, width), 0)
    block = jnp.zeros((16, width), f32)
    for place, row in enumerate(rows):
        block = jnp.where(at == place, row, block)
    return block


def stacked(*blocks):
    return jnp.concatenate([block.astype(bf16) for block in blocks], axis=0)


def norm_parts(value):
    centered = value - jnp.mean(value, axis=1, keepdims=True)
    variance = jnp.mean(centered * centered, axis=1, keepdims=True)
    scale = lax.rsqrt(variance + eps)
    return centered * scale, scale


def norm_back(unit, scale, gain, grad):
    scaled = grad * gain
    along = jnp.mean(scaled * unit, axis=1, keepdims=True)
    return scale * (scaled - jnp.mean(scaled, axis=1, keepdims=True) - unit * along)


def enter_kernel(
    x_ref, gains_ref, w_ref, fq_ref, fk_ref, tail_ref,
    hid_ref, qkv_ref, pq_ref, pk_ref, state_ref, norm_ref, logit_ref,
):
    head_dim, width = fq_ref.shape
    rows = x_ref.shape[0]
    unit, _ = norm_parts(x_ref[...].astype(f32))
    hid = (unit * gains_ref[0:1, :] + gains_ref[1:2, :]).astype(bf16)
    hid_ref[...] = hid.T
    for low in range(0, 3 * width, width):
        qkv_ref[low : low + width, :] = dg(hid, w_ref[:, low : low + width], 1, 0).astype(bf16).T

    @pl.when(pl.program_id(0) == 0)
    def _():
        state_ref[...] = jnp.zeros_like(state_ref)
        norm_ref[...] = jnp.zeros_like(norm_ref)

    heads = width // head_dim
    for low in range(0, width, head_dim):
        high = low + head_dim
        logit_ref[low:high, :] = dg(fq_ref[:, low:high], qkv_ref[low:high, :], 1, 0)
        logit_ref[width + low : width + high, :] = dg(
            fk_ref[:, low:high], qkv_ref[width + low : width + high, :], 1, 0
        )
    step = min(128, rows)
    for part, phi_ref in enumerate((pq_ref, pk_ref)):
        for low in range(0, width, head_dim):
            first = part * width + low
            for lane in range(0, rows, step):
                lanes = slice(lane, lane + step)
                logits = logit_ref[first : first + head_dim, lanes]
                up = jnp.exp(logits - jnp.max(logits, axis=0, keepdims=True))
                low_most = jnp.exp(jnp.min(logits, axis=0, keepdims=True) - logits)
                up = up * (1.0 / jnp.sum(up, axis=0, keepdims=True))
                low_most = low_most * (1.0 / jnp.sum(low_most, axis=0, keepdims=True))
                phi_ref[2 * low : 2 * low + head_dim, lanes] = up.astype(bf16)
                phi_ref[2 * low + head_dim : 2 * low + 2 * head_dim, lanes] = low_most.astype(bf16)
    ones = jnp.ones((16, rows), bf16)
    for head in range(heads):
        low, high = (head * head_dim, (head + 1) * head_dim)
        wide = stacked(qkv_ref[2 * width + low : 2 * width + high, :], ones)
        local = dg(wide, pk_ref[2 * low : 2 * high, :] * tail_ref[...], 1, 1)
        state_ref[low:high, :] += local[:head_dim]
        norm_ref[head : head + 1, :] += local[head_dim : head_dim + 1]


def masked(scores, start, first, offset):
    key_at = lax.broadcasted_iota(jnp.int32, scores.shape, 0) + first
    allowed = key_at >= start
    if first + scores.shape[0] > offset:
        query_at = lax.broadcasted_iota(jnp.int32, scores.shape, 1) + offset
        allowed = allowed & (key_at <= query_at)
    return jnp.where(allowed, scores, 0.0).astype(bf16)


def causal(make, start, low, high):
    blocks = [masked(make(0, low), start, 0, low)] if low else []
    return jnp.concatenate(blocks + [masked(make(low, high), start, low, low)], axis=0)


def local_kernel(pq_ref, pk_ref, v_ref, start_ref, num_ref, den_ref):
    tokens = pq_ref.shape[1]
    head_dim = v_ref.shape[0]
    step = min(256, tokens)
    lows = list(range(0, tokens, step))

    def weights_at(low):
        phi = pq_ref[:, low : low + step]
        make = lambda first, last: dg(pk_ref[:, first:last], phi, 0, 0)
        return causal(make, start_ref[:, low : low + step], low, low + step)

    upcoming = weights_at(lows[-1])
    for at in range(len(lows) - 1, -1, -1):
        weights = upcoming
        low, high = (lows[at], lows[at] + step)
        if at:
            upcoming = weights_at(lows[at - 1])
        wide = stacked(v_ref[:, :high], jnp.ones((16, high), bf16))
        local = dg(wide, weights, 1, 0)
        num_ref[:, low:high] = local[:head_dim]
        den_ref[0, :, low:high] = local[head_dim : head_dim + 1]


def block_kernel(
    num0_ref, num1_ref, den0_ref, den1_ref, pq_ref, state_ref, norm_ref, open_ref, x_ref, cot_ref, gains_ref,
    wout_ref, wfc_ref, wproj_ref,
    low_ref, hid_ref, act_ref, dpre_ref, out_ref, dbranch_ref, dresid_ref, dnum_ref, dden_ref,
    gstate_ref, gnorm_ref, sums_ref,
    mixed_ref, inverse_ref,
):
    width, features = state_ref.shape
    head_dim = features // 2
    rows = x_ref.shape[0]
    opened = open_ref[...]

    @pl.when(pl.program_id(0) == 0)
    def _():
        gstate_ref[...] = jnp.zeros_like(gstate_ref)
        gnorm_ref[...] = jnp.zeros_like(gnorm_ref)
        sums_ref[...] = jnp.zeros_like(sums_ref)

    for head in range(width // head_dim):
        low, high = (head * head_dim, (head + 1) * head_dim)
        state = parts_of(state_ref[low:high, :])
        normer = rows_of(parts_of(norm_ref[head : head + 1, :]), features)
        carry = dg(stacked(*state, normer), pq_ref[2 * low : 2 * high, :], 1, 0)
        half = width // 2
        num_ref, den_ref = (num0_ref, den0_ref) if low < half else (num1_ref, den1_ref)
        num = num_ref[low % half : low % half + head_dim, :]
        num = num + opened * (carry[:head_dim] + carry[head_dim:features])
        den = den_ref[head % (half // head_dim)]
        den = den + opened * (carry[features : features + 1] + carry[features + 1 : features + 2])
        inverse = 1.0 / den
        mixed = num * inverse
        inverse_ref[head : head + 1, :] = inverse
        mixed_ref[low:high, :] = mixed
        low_ref[low:high, :] = mixed.astype(bf16)
    resid = x_ref[...].astype(f32) + dg(low_ref[...], wout_ref[...], 0, 0)
    unit, scale = norm_parts(resid)
    hid = (unit * gains_ref[2:3, :] + gains_ref[3:4, :]).astype(bf16)
    hid_ref[...] = hid.T
    cot = cot_ref[...]
    hidden = wfc_ref.shape[1]
    step = hidden // 4
    root = 0.7978845608028654

    def entering(low):
        pre = dg(hid, wfc_ref[:, low : low + step], 1, 0)
        return pre, dg(cot, wproj_ref[low : low + step, :], 1, 1)

    upcoming = entering(0)
    out, dhid = (resid, None)
    for low in range(0, hidden, step):
        pre, dact = upcoming
        if low + step < hidden:
            upcoming = entering(low + step)
        square = pre * pre
        half = 0.5 + 0.5 * jnp.tanh(pre * (root + (root * 0.044715) * square))
        act = pre * half
        rise = (1.0 - half) * (2.0 * root + (6.0 * root * 0.044715) * square)
        dpre = (dact * (half + act * rise)).astype(bf16)
        act = act.astype(bf16)
        act_ref[:, low : low + step] = act
        dpre_ref[:, low : low + step] = dpre
        out = out + dg(act, wproj_ref[low : low + step, :], 1, 0)
        local = dg(dpre, wfc_ref[:, low : low + step], 1, 1)
        dhid = local if dhid is None else dhid + local
    out_ref[...] = out.astype(bf16)
    sums_ref[0:1, :] += jnp.sum(dhid * unit, axis=0, keepdims=True)
    sums_ref[1:2, :] += jnp.sum(dhid, axis=0, keepdims=True)
    dresid = cot.astype(f32) + norm_back(unit, scale, gains_ref[2:3, :], dhid)
    dresid_ref[...] = dresid
    dbranch = dresid.astype(bf16)
    dbranch_ref[...] = dbranch
    dmixed_all = dg(wout_ref[...], dbranch, 1, 1)
    for head in range(width // head_dim):
        low, high = (head * head_dim, (head + 1) * head_dim)
        dmixed = dmixed_all[low:high]
        inverse = inverse_ref[head : head + 1, :]
        dnum = dmixed * inverse
        dden = -jnp.sum(dmixed * mixed_ref[low:high, :], axis=0, keepdims=True) * inverse
        dnum_ref[low:high, :] = dnum
        dden_ref[head] = dden
        wide = stacked(*parts_of(dnum * opened), rows_of(parts_of(dden * opened), rows))
        local = dg(wide, pq_ref[2 * low : 2 * high, :], 1, 1)
        gstate_ref[low:high, :] += local[:head_dim] + local[head_dim:features]
        gnorm_ref[head : head + 1, :] += local[features : features + 1] + local[features + 1 : features + 2]


def logit_back(phi, dphi):
    half = phi.shape[0] // 2
    up, down = (phi[:half].astype(f32), phi[half:].astype(f32))
    dup, ddown = (dphi[:half], dphi[half:])
    dup = dup - jnp.sum(dup * up, axis=0, keepdims=True)
    ddown = ddown - jnp.sum(ddown * down, axis=0, keepdims=True)
    return (up * dup - down * ddown).astype(bf16)


def local_back_kernel(
    pq_ref, pk_ref, q_ref, v_ref, dnum_ref, dden_ref, start_ref, open_ref, state_ref, norm_ref, fq_ref,
    dq_ref, gfq_ref, dphik_ref, dv_ref,
):
    tokens = pq_ref.shape[1]
    features = pq_ref.shape[0]
    step = min(256, tokens)
    state_high, state_low = parts_of(state_ref[...])
    norm_high, norm_low = parts_of(norm_ref[0])
    carried = stacked(
        state_high, state_high, state_low, rows_of((norm_high, norm_high, norm_low), features)
    )
    maps = fq_ref[...]
    gfq = jnp.zeros(gfq_ref.shape[1:], f32)
    lows = list(range(0, tokens, step))

    def weights_at(low):
        high = low + step
        start = start_ref[:, low:high]
        phi = pq_ref[:, low:high]
        dnum_low = dnum_ref[:, low:high].astype(bf16)
        dden = dden_ref[0, :, low:high]
        plain = lambda first, last: dg(pk_ref[:, first:last], phi, 0, 0)
        slope = lambda first, last: dg(v_ref[:, first:last], dnum_low, 0, 0) + dden
        return causal(plain, start, low, high), causal(slope, start, low, high)

    upcoming = weights_at(lows[-1])
    for at in range(len(lows) - 1, -1, -1):
        low, high = (lows[at], lows[at] + step)
        weights, dweights = upcoming
        if at:
            upcoming = weights_at(lows[at - 1])
        phi = pq_ref[:, low:high]
        num_high, num_low = parts_of(dnum_ref[:, low:high])
        dden = dden_ref[0, :, low:high]
        dv = dg(num_high.astype(bf16), weights, 1, 1)
        dphik = dg(phi, dweights, 1, 1)
        if at == len(lows) - 1:
            dv_ref[...] = dv
            dphik_ref[...] = dphik
        else:
            dv_ref[:, :high] += dv
            dphik_ref[:, :high] += dphik
        den_high, den_low = parts_of(dden)
        arriving = stacked(num_high, num_low, num_high, rows_of((den_high, den_low, den_high), step))
        dphi = dg(pk_ref[:, :high], dweights, 1, 0)
        dphi = dphi + open_ref[:, low:high] * dg(carried, arriving, 0, 0)
        dlogit = logit_back(phi, dphi)
        gfq = gfq + dg(q_ref[:, low:high], dlogit, 1, 1)
        dq_ref[:, low:high] = dg(maps, dlogit, 1, 0).astype(bf16)
    gfq_ref[0] = gfq


def key_back_kernel(
    pk_ref, k_ref, v_ref, dphik0_ref, dphik1_ref, dv0_ref, dv1_ref, tail_ref, state_ref, norm_ref, fk_ref,
    dkv_ref, gfk_ref,
):
    features, tokens = pk_ref.shape
    head_dim = features // 2
    state_high, state_low = parts_of(state_ref[...])
    carried = stacked(state_high, state_low, rows_of(parts_of(norm_ref[0]), features))
    values = v_ref[...]
    tail = tail_ref[...]
    wide = stacked(values, values, jnp.ones((16, tokens), bf16))
    phi = pk_ref[...]
    early = pl.program_id(0) < pl.num_programs(0) // 2
    dphi = jnp.where(early, dphik0_ref[...], dphik1_ref[...]) + tail * dg(carried, wide, 0, 0)
    both = dg(stacked(state_high, state_low), phi, 1, 0)
    dv = jnp.where(early, dv0_ref[...], dv1_ref[...]) + tail * (both[:head_dim] + both[head_dim:])
    dlogit = logit_back(phi, dphi)
    gfk_ref[0] = dg(k_ref[...], dlogit, 1, 1)
    dkv_ref[0] = dg(fk_ref[...], dlogit, 1, 0).astype(bf16)
    dkv_ref[1] = dv.astype(bf16)


def leave_kernel(dq0_ref, dq1_ref, dkv_ref, w_ref, x_ref, gains_ref, dresid_ref, grad_ref, sums_ref):
    width = x_ref.shape[1]

    @pl.when(pl.program_id(0) == 0)
    def _():
        sums_ref[...] = jnp.zeros_like(sums_ref)

    dq = jnp.concatenate([dq0_ref[...], dq1_ref[...]], axis=0)
    dhid = dg(dq, w_ref[:, :width], 0, 1)
    dhid = dhid + dg(dkv_ref[0], w_ref[:, width : 2 * width], 0, 1)
    dhid = dhid + dg(dkv_ref[1], w_ref[:, 2 * width :], 0, 1)
    unit, scale = norm_parts(x_ref[...].astype(f32))
    sums_ref[0:1, :] += jnp.sum(dhid * unit, axis=0, keepdims=True)
    sums_ref[1:2, :] += jnp.sum(dhid, axis=0, keepdims=True)
    grad_ref[...] = dresid_ref[...] + norm_back(unit, scale, gains_ref[0:1, :], dhid)


def whole(shape):
    return pl.BlockSpec(shape, lambda i: (0,) * len(shape))


def down(rows, width):
    return pl.BlockSpec((rows, width), lambda i: (i, 0))


def across(rows, width):
    return pl.BlockSpec((rows, width), lambda i: (0, i))


def heads_across(heads, width):
    return pl.BlockSpec((heads, 1, width), lambda i: (0, 0, i))


def one_head(width, first=0):
    return pl.BlockSpec((1, 1, width), lambda i: (first + i, 0, 0))


def head_rows(rows, width, first=0):
    return pl.BlockSpec((rows, width), lambda i: (first + i, 0))


def shape_of(shape, dtype):
    return jax.ShapeDtypeStruct(shape, dtype)


def call(kernel, grid, ins, outs, shapes, args, scratch=()):
    return pl.pallas_call(
        kernel,
        grid=(grid,),
        in_specs=ins,
        out_specs=outs,
        out_shape=shapes,
        scratch_shapes=list(scratch),
        compiler_params=pltpu.CompilerParams(
            dimension_semantics=("arbitrary",), vmem_limit_bytes=grant
        ),
    )(*args)


def log2_of(count):
    return count.bit_length() - 1


def sizes():
    return (lax.axis_size("grp"), lax.axis_size("tok"))


def place_of():
    return lax.axis_index("grp") * lax.axis_size("tok") + lax.axis_index("tok")


def flips(first, second):
    grp_size, tok_size = sizes()
    pairs = []
    for place in range(grp_size * tok_size):
        pairs.append((place, place ^ (second if (place // tok_size) % 2 else first)))
    return pairs


def far_flips():
    grp_size, tok_size = sizes()
    return [(2 * tok_size) << bit for bit in range(log2_of(grp_size) - 1)]


def order_of(turn):
    tok_bits = [1 << bit for bit in range(log2_of(lax.axis_size("tok")))]
    near = far_flips() + tok_bits[:-1]
    turn = turn % len(near)
    return near[turn:] + near[:turn] + tok_bits[-1:]


def slots_of(turn):
    grp_size, tok_size = sizes()
    order = order_of(turn)
    slots = []
    for tok in range(tok_size):
        for far in range(grp_size // 2):
            place = far * 2 * tok_size + tok
            bits = [(place // flip) % 2 for flip in order]
            slots.append(sum(bit << (len(bits) - 1 - at) for at, bit in enumerate(bits)))
    return jnp.array(slots, jnp.int32)


def tables_of(turns):
    core = lax.axis_index("grp") % 2
    own = lax.axis_index("tok") * (lax.axis_size("grp") // 2) + lax.axis_index("grp") // 2
    even, odd = (slots_of(turns[0]), slots_of(turns[1]))
    mine = jnp.where(core == 0, even, odd)
    theirs = jnp.where(core == 0, odd, even)
    return jnp.concatenate([theirs ^ theirs[own], mine ^ mine[own], core[None].astype(jnp.int32)])


def product_kernel(counts, theirs, mine, by_columns, table_ref, *refs):
    count, tails = counts
    ins, refs = (refs[:count], refs[count:])
    tail_refs, refs = (refs[:tails], refs[tails:])
    theirs_ref, keep_ref, give_ref = refs
    pieces = (table_ref.shape[0] - 1) // 2
    half = pieces // 2
    rows, lanes = theirs_ref.shape[1:]
    for turn, forms in enumerate((theirs, mine)):
        at = 0
        blocks = []
        for left, right, left_dim, right_dim in forms:
            right = ins[right][...]
            value = dg(ins[left][...], right.reshape(right.shape[-2:]), left_dim, right_dim)
            blocks.append((at, value))
            at += value.shape[1]
        if tails:
            blocks.append((at, tail_refs[turn][0]))
        base = turn * pieces
        cuts = []
        for column, value in blocks:
            if by_columns:
                far = value.shape[0] // rows
                for tok in range(value.shape[1] // lanes):
                    for place in range(far):
                        part = value[place * rows : (place + 1) * rows, tok * lanes : (tok + 1) * lanes]
                        cuts.append((tok * far + place, slice(0, lanes), part))
                base = turn * pieces + pl.program_id(0) * len(cuts)
            else:
                for piece in range(value.shape[0] // rows):
                    part = value[piece * rows : (piece + 1) * rows]
                    cuts.append((piece, slice(column, column + value.shape[1]), part))
        for piece, span, part in cuts:
            slot = table_ref[base + piece]
            if turn == 0:
                theirs_ref[slot, :, span] = part
                continue

            @pl.when(slot < half)
            def _(part=part, span=span, slot=slot):
                keep_ref[slot, :, span] = part

            @pl.when(slot >= half)
            def _(part=part, span=span, slot=slot):
                give_ref[slot - half, :, span] = part


def products(table, theirs, mine, ins, specs, grid, piece, tail=None, by_columns=False):
    pieces = (table.shape[0] - 1) // 2
    if by_columns or grid == 1:
        block = lambda count: pl.BlockSpec((count,) + piece, lambda i, t: (0, 0, 0))
    else:
        block = lambda count: pl.BlockSpec((count, piece[0], piece[1] // grid), lambda i, t: (0, 0, i))
    specs = list(specs)
    ins = list(ins)
    count = len(ins)
    if tail is not None:
        ins += [tail, tail]
        specs.append(pl.BlockSpec((1,) + tail.shape[1:], lambda i, t: (1 - t[2 * pieces], 0, 0)))
        specs.append(pl.BlockSpec((1,) + tail.shape[1:], lambda i, t: (t[2 * pieces], 0, 0)))
    counts = (pieces, pieces // 2, pieces // 2)
    return pl.pallas_call(
        partial(product_kernel, (count, len(ins) - count), theirs, mine, by_columns),
        grid_spec=pltpu.PrefetchScalarGridSpec(
            num_scalar_prefetch=1, grid=(grid,), in_specs=specs, out_specs=[block(c) for c in counts]
        ),
        out_shape=[shape_of((c,) + piece, f32) for c in counts],
        compiler_params=pltpu.CompilerParams(
            dimension_semantics=("arbitrary",), vmem_limit_bytes=grant
        ),
    )(table, *ins)


def send(value, first, second):
    return lax.ppermute(value, ("grp", "tok"), flips(first, second))


def swap_cores(value):
    tok_size = lax.axis_size("tok")
    return send(value, tok_size, tok_size)


def fold(keep, give, other, turns):
    orders = (order_of(turns[0]), order_of(turns[1]))
    count = keep.shape[0]
    give = give + other[count:]
    other = other[:count]
    for at, (even, odd) in enumerate(zip(*orders)):
        landed = send(give, even, odd)
        half = keep.shape[0] // 2
        if at == 0:
            landed_of = lambda low, high: landed[low:high] + other[low:high]
        else:
            landed_of = lambda low, high: landed[low:high]
        if half:
            give = keep[half:] + landed_of(half, 2 * half)
            keep = keep[:half] + landed_of(0, half)
        else:
            keep = keep + landed_of(0, 1)
    for flip in far_flips():
        bit = (place_of() & flip) != 0
        landed = send(keep, flip, flip)
        keep = jnp.concatenate(
            [jnp.where(bit, landed, keep), jnp.where(bit, keep, landed)], axis=0
        )
    keep = keep.reshape(-1, keep.shape[2])
    landed = swap_cores(keep)
    core = lax.axis_index("grp") % 2
    return (jnp.where(core == 0, keep, landed), jnp.where(core == 0, landed, keep))


def chain_kernel(backward, got_ref, out_ref):
    count, rows, lanes = got_ref.shape

    def step(at, so_far):
        block = count - 1 - at if backward else at
        out_ref[block] = so_far
        local = got_ref[block]
        return local + local[rows - 1 :, lanes - 1 :] * so_far

    lax.fori_loop(0, count, step, jnp.zeros((rows, lanes), f32), unroll=8)


def carry_scan(state, norm, keep, backward):
    grp_size, tok_size = sizes()
    count = grp_size * tok_size
    lanes = state.shape[1]
    share = state.shape[0] // count
    spare = norm.size // count
    extra = jnp.concatenate(
        [norm.reshape(count, spare), jnp.zeros((count, lanes - 1 - spare), f32), jnp.full((count, 1), keep)],
        axis=1,
    )
    packed = jnp.concatenate([state.reshape(count, share, lanes), extra[:, None]], axis=1)
    landed = lax.all_to_all(packed, ("grp", "tok"), 0, 0, tiled=True)
    summed = pl.pallas_call(
        partial(chain_kernel, backward),
        out_shape=shape_of(landed.shape, f32),
        compiler_params=pltpu.CompilerParams(vmem_limit_bytes=grant),
    )(landed)
    home = lax.all_to_all(summed, ("grp", "tok"), 0, 0, tiled=True)
    return home[:, :share].reshape(state.shape), home[:, share, :spare].reshape(norm.shape)


def reduce_vectors(stack):
    grp_size, tok_size = sizes()
    count, length = stack.shape
    share = length // tok_size
    blocks = stack.reshape(count, tok_size, share).transpose(1, 0, 2)
    blocks = blocks.reshape(tok_size, count * share)
    spread = jnp.broadcast_to(blocks[None], (grp_size,) + blocks.shape)
    spread = spread.reshape(grp_size * tok_size, count * share)
    landed = lax.all_to_all(spread, ("grp", "tok"), 0, 0, tiled=True)
    return jnp.sum(landed, axis=0).reshape(count, share)


def on_device(
    layer_input,
    doc_starts,
    ln1_gain,
    ln1_shift,
    w_qkv,
    feat_q,
    feat_k,
    w_out,
    ln2_gain,
    ln2_shift,
    w_fc,
    w_proj,
    cotangent,
):
    tokens, width = layer_input.shape
    head_dim = feat_q.shape[1]
    heads = width // head_dim
    feats = 2 * head_dim
    hidden = w_fc.shape[1]
    rows = min(256, tokens)
    blocks = tokens // rows
    gains = jnp.stack([ln1_gain, ln1_shift, ln2_gain, ln2_shift])

    at = jnp.arange(tokens, dtype=jnp.int32)
    marked = (doc_starts[:, None] > 0) & (at[:, None] <= at[None, :])
    last = jnp.max(jnp.where(marked, at[:, None], -1), axis=0)
    start = jnp.maximum(last, 0)[None]
    opened = (last < 0).astype(f32)[None]
    tail = (at >= last[-1]).astype(f32)[None]
    keep = (last[-1] < 0).astype(f32)

    hid1, qkv, phi_q, phi_k, state, norm = call(
        enter_kernel, blocks,
        [down(rows, width), whole((4, width)), whole(w_qkv.shape),
         whole((head_dim, width)), whole((head_dim, width)), across(1, rows)],
        [across(width, rows), across(3 * width, rows), across(2 * width, rows), across(2 * width, rows),
         whole((width, feats)), whole((heads, feats))],
        [shape_of((width, tokens), bf16), shape_of((3 * width, tokens), bf16),
         shape_of((2 * width, tokens), bf16), shape_of((2 * width, tokens), bf16),
         shape_of((width, feats), f32), shape_of((heads, feats), f32)],
        (layer_input, gains, w_qkv, feat_q.T, feat_k.T, tail.astype(bf16)),
        [pltpu.VMEM((2 * width, rows), f32)],
    )
    state_in, norm_in = carry_scan(state, norm, keep, False)
    part = heads // 2
    locals_ = [
        call(
            local_kernel, part,
            [head_rows(feats, tokens, at * part), head_rows(feats, tokens, at * part),
             head_rows(head_dim, tokens, 2 * heads + at * part), whole((1, tokens))],
            [head_rows(head_dim, tokens), one_head(tokens)],
            [shape_of((width // 2, tokens), f32), shape_of((part, 1, tokens), f32)],
            (phi_q, phi_k, qkv, start),
        )
        for at in range(2)
    ]
    once = lambda shape: pl.BlockSpec(shape, lambda i: (0, 0), pipeline_mode=pl.Buffered(1))
    mixed_low, hid2, act, dpre, output, dbranch, dresid, dnum, dden, back_state, back_norm, sums2 = call(
        block_kernel, blocks,
        [across(width // 2, rows), across(width // 2, rows), heads_across(part, rows),
         heads_across(part, rows), across(2 * width, rows), whole((width, feats)),
         whole((heads, feats)), across(1, rows), down(rows, width), down(rows, width), whole((4, width)),
         once(w_out.shape), once(w_fc.shape), once(w_proj.shape)],
        [across(width, rows), across(width, rows), down(rows, hidden), down(rows, hidden),
         down(rows, width), down(rows, width), down(rows, width), across(width, rows),
         heads_across(heads, rows), whole((width, feats)), whole((heads, feats)), whole((8, width))],
        [shape_of((width, tokens), bf16), shape_of((width, tokens), bf16), shape_of((tokens, hidden), bf16),
         shape_of((tokens, hidden), bf16), shape_of((tokens, width), bf16), shape_of((tokens, width), bf16),
         shape_of((tokens, width), f32), shape_of((width, tokens), f32), shape_of((heads, 1, tokens), f32),
         shape_of((width, feats), f32), shape_of((heads, feats), f32), shape_of((8, width), f32)],
        (locals_[0][0], locals_[1][0], locals_[0][1], locals_[1][1], phi_q, state_in, norm_in, opened,
         layer_input, cotangent, gains, w_out, w_fc, w_proj),
        [pltpu.VMEM((width, rows), f32), pltpu.VMEM((16, rows), f32)],
    )
    half = width // 2
    fars, toks = (lax.axis_size("grp") // 2, lax.axis_size("tok"))
    piece_rows = width // (fars * toks)
    turns_a, turns_b, turns_c, turns_d = ((0, 1), (2, 0), (1, 2), (0, 1))
    table_a, table_b, table_c, table_d = map(tables_of, (turns_a, turns_b, turns_c, turns_d))
    last_at = table_a.shape[0] - 1
    plain = lambda rows_: pl.BlockSpec((rows_, tokens), lambda i, t: (0, 0))
    which = lambda turn, t: t[last_at] if turn else 1 - t[last_at]
    right_half = lambda turn: pl.BlockSpec((tokens, half), lambda i, t: (0, which(turn, t)))
    chosen = lambda row, turn: pl.BlockSpec((1, half, tokens), lambda i, t: (row, which(turn, t), 0))
    quarter = lambda turn: pl.BlockSpec((tokens, hidden // 8), lambda i, t: (0, 4 * which(turn, t) + i))
    theirs_a, keep_a, give_a = products(
        table_a, ((0, 2, 0, 0),), ((1, 2, 0, 0),), (cotangent, cotangent, act),
        (right_half(0), right_half(1), pl.BlockSpec((tokens, hidden // 4), lambda i, t: (0, i))),
        4, (half // fars, hidden // toks), None, True,
    )
    other_a = swap_cores(theirs_a)
    theirs_b, keep_b, give_b = products(
        table_b, ((0, 1, 1, 0),), ((0, 2, 1, 0),), (hid2, dpre, dpre),
        (plain(width), quarter(0), quarter(1)), 4, (piece_rows, hidden // 2),
    )
    other_b = swap_cores(theirs_b)
    state_back, norm_back_in = carry_scan(back_state, back_norm, keep, True)
    split = [
        call(
            local_back_kernel, part,
            [head_rows(feats, tokens, at * part), head_rows(feats, tokens, at * part),
             head_rows(head_dim, tokens, at * part), head_rows(head_dim, tokens, 2 * heads + at * part),
             head_rows(head_dim, tokens, at * part), one_head(tokens, at * part),
             whole((1, tokens)), whole((1, tokens)), head_rows(head_dim, feats, at * part),
             one_head(feats, at * part), head_rows(head_dim, head_dim, at * part)],
            [head_rows(head_dim, tokens), pl.BlockSpec((1, head_dim, head_dim), lambda i: (i, 0, 0)),
             head_rows(feats, tokens), head_rows(head_dim, tokens)],
            [shape_of((width // 2, tokens), bf16), shape_of((part, head_dim, head_dim), f32),
             shape_of((width, tokens), f32), shape_of((width // 2, tokens), f32)],
            (phi_q, phi_k, qkv, qkv, dnum, dden, start, opened, state_in, norm_in[:, None], feat_q),
        )
        for at in range(2)
    ]
    gfq = jnp.concatenate([split[0][1], split[1][1]], axis=0)
    lower = lambda rows_: pl.BlockSpec((rows_, tokens), lambda i: (jnp.minimum(i, part - 1), 0))
    upper = lambda rows_: pl.BlockSpec((rows_, tokens), lambda i: (jnp.maximum(i - part, 0), 0))
    dkv, gfk = call(
        key_back_kernel, heads,
        [head_rows(feats, tokens), head_rows(head_dim, tokens, heads),
         head_rows(head_dim, tokens, 2 * heads), lower(feats), upper(feats), lower(head_dim), upper(head_dim),
         whole((1, tokens)), head_rows(head_dim, feats), one_head(feats), head_rows(head_dim, head_dim)],
        [pl.BlockSpec((2, head_dim, tokens), lambda i: (0, i, 0)),
         pl.BlockSpec((1, head_dim, head_dim), lambda i: (i, 0, 0))],
        [shape_of((2, width, tokens), bf16), shape_of((heads, head_dim, head_dim), f32)],
        (phi_k, qkv, qkv, split[0][2], split[1][2], split[0][3], split[1][3], tail, state_back, norm_back_in[:, None], feat_k),
    )
    grad_input, sums1 = call(
        leave_kernel, blocks,
        [across(width // 2, rows), across(width // 2, rows),
         pl.BlockSpec((2, width, rows), lambda i: (0, 0, i)), whole(w_qkv.shape),
         down(rows, width), whole((4, width)), down(rows, width)],
        [down(rows, width), whole((8, width))],
        [shape_of((tokens, width), f32), shape_of((8, width), f32)],
        (split[0][0], split[1][0], dkv, w_qkv, layer_input, gains, dresid),
    )

    first_core = lax.axis_index("grp") % 2 == 0
    theirs_q = jnp.where(first_core, split[1][0], split[0][0])
    mine_q = jnp.where(first_core, split[0][0], split[1][0])
    theirs_c, keep_c, give_c = products(
        table_c, ((0, 1, 1, 0), (3, 4, 1, 1)), ((0, 2, 1, 0), (3, 5, 1, 1)),
        (mixed_low, dbranch, dbranch, hid1, theirs_q, mine_q),
        (plain(width), right_half(0), right_half(1), plain(width), plain(half), plain(half)),
        1, (piece_rows, 2 * half),
    )
    other_c = swap_cores(theirs_c)
    feats_both = jnp.stack([gfq.reshape(width, head_dim), gfk.reshape(width, head_dim)])
    feats_both = jnp.pad(feats_both, ((0, 0), (0, 0), (0, feats - head_dim)))

    theirs_d, keep_d, give_d = products(
        table_d, ((0, 1, 1, 1), (0, 2, 1, 1)), ((0, 3, 1, 1), (0, 4, 1, 1)),
        (hid1, dkv, dkv, dkv, dkv),
        (plain(width), chosen(0, 0), chosen(1, 0), chosen(0, 1), chosen(1, 1)),
        1, (piece_rows, 2 * half + feats), feats_both,
    )
    other_d = swap_cores(theirs_d)
    vectors = reduce_vectors(jnp.concatenate([sums1[:2], sums2[:2]], axis=0))
    grad_proj = jnp.concatenate(fold(keep_a, give_a, other_a, turns_a), axis=0).T
    grad_fc = jnp.concatenate(fold(keep_b, give_b, other_b, turns_b), axis=1)
    c_pair = fold(keep_c, give_c, other_c, turns_c)
    d_pair = fold(keep_d, give_d, other_d, turns_d)
    grad_out = jnp.concatenate([part[:, :half] for part in c_pair], axis=1)
    grad_qkv = jnp.concatenate(
        [part[:, half:] for part in c_pair]
        + [part[:, :half] for part in d_pair]
        + [part[:, half : 2 * half] for part in d_pair],
        axis=1,
    )
    return (
        output,
        grad_input,
        vectors[0],
        vectors[1],
        grad_qkv,
        d_pair[0][:, 2 * half : 2 * half + head_dim],
        d_pair[1][:, 2 * half : 2 * half + head_dim],
        grad_out,
        vectors[2],
        vectors[3],
        grad_fc,
        grad_proj,
    )


def solution(mesh):
    in_specs = (
        P(("grp", "tok"), None),
        P(("grp", "tok")),
        P(),
        P(),
        P(),
        P(),
        P(),
        P(),
        P(),
        P(),
        P(),
        P(),
        P(("grp", "tok"), None),
    )
    out_specs = (
        P(("grp", "tok"), None),
        P(("grp", "tok"), None),
        P("tok"),
        P("tok"),
        P("tok", None),
        P("tok", None),
        P("tok", None),
        P("tok", None),
        P("tok"),
        P("tok"),
        P("tok", None),
        P("tok", None),
    )

    return jax.shard_map(on_device, mesh=mesh, in_specs=in_specs, out_specs=out_specs, check_vma=False)
```

```python
from functools import partial

import jax
import jax.numpy as jnp
from jax import lax
from jax.experimental import pallas as pl
from jax.experimental.pallas import tpu as pltpu
from jax.sharding import PartitionSpec as P


eps = 1e-05
f32 = jnp.float32
bf16 = jnp.bfloat16
grant = 58 * 1024 * 1024


def dg(left, right, left_dim, right_dim):
    dims = (((left_dim,), (right_dim,)), ((), ()))
    return lax.dot_general(left, right, dims, preferred_element_type=f32)


def parts_of(value):
    high = value.astype(bf16).astype(f32)
    return high, value - high


def rows_of(rows, width):
    at = lax.broadcasted_iota(jnp.int32, (16, width), 0)
    block = jnp.zeros((16, width), f32)
    for place, row in enumerate(rows):
        block = jnp.where(at == place, row, block)
    return block


def stacked(*blocks):
    return jnp.concatenate([block.astype(bf16) for block in blocks], axis=0)


def norm_parts(value):
    centered = value - jnp.mean(value, axis=1, keepdims=True)
    variance = jnp.mean(centered * centered, axis=1, keepdims=True)
    scale = lax.rsqrt(variance + eps)
    return centered * scale, scale


def norm_back(unit, scale, gain, grad):
    scaled = grad * gain
    along = jnp.mean(scaled * unit, axis=1, keepdims=True)
    return scale * (scaled - jnp.mean(scaled, axis=1, keepdims=True) - unit * along)


def last_start(starts_ref):
    starts = starts_ref[...]
    at = lax.broadcasted_iota(jnp.int32, starts.shape, 1)
    return jnp.max(jnp.where(starts > 0, at, -1), axis=1, keepdims=True)


def pack_carry(packed_ref, state_ref, norm_ref, last):
    count, rows, lanes = packed_ref.shape
    share = rows - 2
    keep = jnp.broadcast_to(jnp.where(last < 0, 1.0, 0.0), (1, lanes))
    for place in range(count):
        packed_ref[place, :share, :] = state_ref[place * share : (place + 1) * share, :]
        row = norm_ref[place : place + 1, :] if place < norm_ref.shape[0] else jnp.zeros((1, lanes), f32)
        packed_ref[place, share : share + 1, :] = row
        packed_ref[place, share + 1 :, :] = keep


def unpack_carry(packed_ref, state_ref, norm_ref):
    count, rows, _ = packed_ref.shape
    share = rows - 2
    for place in range(count):
        state_ref[place * share : (place + 1) * share, :] = packed_ref[place, :share, :]
    for place in range(norm_ref.shape[0]):
        norm_ref[place : place + 1, :] = packed_ref[place, share : share + 1, :]


def enter_kernel(
    x_ref, gains_ref, w_ref, fq_ref, fk_ref, starts_ref,
    hid_ref, qkv_ref, pq_ref, pk_ref, packed_ref, logit_ref, state_ref, norm_ref,
):
    head_dim, width = fq_ref.shape
    rows = x_ref.shape[0]
    last = last_start(starts_ref)
    at = lax.broadcasted_iota(jnp.int32, (1, rows), 1) + pl.program_id(0) * rows
    tail = jnp.where(at >= last, 1.0, 0.0).astype(bf16)
    unit, _ = norm_parts(x_ref[...].astype(f32))
    hid = (unit * gains_ref[0:1, :] + gains_ref[1:2, :]).astype(bf16)
    hid_ref[...] = hid.T
    for low in range(0, 3 * width, width):
        qkv_ref[low : low + width, :] = dg(hid, w_ref[:, low : low + width], 1, 0).astype(bf16).T

    @pl.when(pl.program_id(0) == 0)
    def _():
        state_ref[...] = jnp.zeros_like(state_ref)
        norm_ref[...] = jnp.zeros_like(norm_ref)

    heads = width // head_dim
    for low in range(0, width, head_dim):
        high = low + head_dim
        logit_ref[low:high, :] = dg(fq_ref[:, low:high], qkv_ref[low:high, :], 1, 0)
        logit_ref[width + low : width + high, :] = dg(
            fk_ref[:, low:high], qkv_ref[width + low : width + high, :], 1, 0
        )
    step = min(128, rows)
    for part, phi_ref in enumerate((pq_ref, pk_ref)):
        for low in range(0, width, head_dim):
            first = part * width + low
            for lane in range(0, rows, step):
                lanes = slice(lane, lane + step)
                logits = logit_ref[first : first + head_dim, lanes]
                up = jnp.exp(logits - jnp.max(logits, axis=0, keepdims=True))
                low_most = jnp.exp(jnp.min(logits, axis=0, keepdims=True) - logits)
                up = up * (1.0 / jnp.sum(up, axis=0, keepdims=True))
                low_most = low_most * (1.0 / jnp.sum(low_most, axis=0, keepdims=True))
                phi_ref[2 * low : 2 * low + head_dim, lanes] = up.astype(bf16)
                phi_ref[2 * low + head_dim : 2 * low + 2 * head_dim, lanes] = low_most.astype(bf16)
    ones = jnp.ones((16, rows), bf16)
    for head in range(heads):
        low, high = (head * head_dim, (head + 1) * head_dim)
        wide = stacked(qkv_ref[2 * width + low : 2 * width + high, :], ones)
        local = dg(wide, pk_ref[2 * low : 2 * high, :] * tail, 1, 1)
        state_ref[low:high, :] += local[:head_dim]
        norm_ref[head : head + 1, :] += local[head_dim : head_dim + 1]

    @pl.when(pl.program_id(0) == pl.num_programs(0) - 1)
    def _():
        pack_carry(packed_ref, state_ref, norm_ref, last)


def masked(scores, start, first, offset):
    key_at = lax.broadcasted_iota(jnp.int32, scores.shape, 0) + first
    allowed = key_at >= start
    if first + scores.shape[0] > offset:
        query_at = lax.broadcasted_iota(jnp.int32, scores.shape, 1) + offset
        allowed = allowed & (key_at <= query_at)
    return jnp.where(allowed, scores, 0.0).astype(bf16)


def causal(make, start, low, high):
    blocks = [masked(make(0, low), start, 0, low)] if low else []
    return jnp.concatenate(blocks + [masked(make(low, high), start, low, low)], axis=0)


def local_kernel(pq_ref, pk_ref, v_ref, start_ref, num_ref, den_ref):
    tokens = pq_ref.shape[1]
    head_dim = v_ref.shape[0]
    step = min(256, tokens)
    lows = list(range(0, tokens, step))

    def weights_at(low):
        phi = pq_ref[:, low : low + step]
        make = lambda first, last: dg(pk_ref[:, first:last], phi, 0, 0)
        return causal(make, start_ref[:, low : low + step], low, low + step)

    upcoming = weights_at(lows[-1])
    for at in range(len(lows) - 1, -1, -1):
        weights = upcoming
        low, high = (lows[at], lows[at] + step)
        if at:
            upcoming = weights_at(lows[at - 1])
        wide = stacked(v_ref[:, :high], jnp.ones((16, high), bf16))
        local = dg(wide, weights, 1, 0)
        num_ref[:, low:high] = local[:head_dim]
        den_ref[0, :, low:high] = local[head_dim : head_dim + 1]


def block_kernel(
    num0_ref, num1_ref, den0_ref, den1_ref, pq_ref, home_ref, starts_ref, open_ref, x_ref, cot_ref, gains_ref,
    wout_ref, wfc_ref, wproj_ref,
    low_ref, hid_ref, act_ref, dpre_ref, out_ref, dbranch_ref, dresid_ref, dnum_ref, dden_ref,
    packed_ref, sums_ref, state_ref, norms_ref,
    mixed_ref, inverse_ref, norm_ref, gstate_ref, gnorm_ref,
):
    width, features = state_ref.shape
    head_dim = features // 2
    rows = x_ref.shape[0]
    opened = open_ref[...]

    @pl.when(pl.program_id(0) == 0)
    def _():
        unpack_carry(home_ref, state_ref, norm_ref)
        for head in range(norm_ref.shape[0]):
            norms_ref[head] = norm_ref[head : head + 1, :]
        gstate_ref[...] = jnp.zeros_like(gstate_ref)
        gnorm_ref[...] = jnp.zeros_like(gnorm_ref)
        sums_ref[...] = jnp.zeros_like(sums_ref)

    for head in range(width // head_dim):
        low, high = (head * head_dim, (head + 1) * head_dim)
        state = parts_of(state_ref[low:high, :])
        normer = rows_of(parts_of(norm_ref[head : head + 1, :]), features)
        carry = dg(stacked(*state, normer), pq_ref[2 * low : 2 * high, :], 1, 0)
        half = width // 2
        num_ref, den_ref = (num0_ref, den0_ref) if low < half else (num1_ref, den1_ref)
        num = num_ref[low % half : low % half + head_dim, :]
        num = num + opened * (carry[:head_dim] + carry[head_dim:features])
        den = den_ref[head % (half // head_dim)]
        den = den + opened * (carry[features : features + 1] + carry[features + 1 : features + 2])
        inverse = 1.0 / den
        mixed = num * inverse
        inverse_ref[head : head + 1, :] = inverse
        mixed_ref[low:high, :] = mixed
        low_ref[low:high, :] = mixed.astype(bf16)
    resid = x_ref[...].astype(f32) + dg(low_ref[...], wout_ref[...], 0, 0)
    unit, scale = norm_parts(resid)
    hid = (unit * gains_ref[2:3, :] + gains_ref[3:4, :]).astype(bf16)
    hid_ref[...] = hid.T
    cot = cot_ref[...]
    hidden = wfc_ref.shape[1]
    step = hidden // 4
    root = 0.7978845608028654

    def entering(low):
        pre = dg(hid, wfc_ref[:, low : low + step], 1, 0)
        return pre, dg(cot, wproj_ref[low : low + step, :], 1, 1)

    upcoming = entering(0)
    out, dhid = (resid, None)
    for low in range(0, hidden, step):
        pre, dact = upcoming
        if low + step < hidden:
            upcoming = entering(low + step)
        square = pre * pre
        half = 0.5 + 0.5 * jnp.tanh(pre * (root + (root * 0.044715) * square))
        act = pre * half
        rise = (1.0 - half) * (2.0 * root + (6.0 * root * 0.044715) * square)
        dpre = (dact * (half + act * rise)).astype(bf16)
        act = act.astype(bf16)
        act_ref[:, low : low + step] = act
        dpre_ref[:, low : low + step] = dpre
        out = out + dg(act, wproj_ref[low : low + step, :], 1, 0)
        local = dg(dpre, wfc_ref[:, low : low + step], 1, 1)
        dhid = local if dhid is None else dhid + local
    out_ref[...] = out.astype(bf16)
    sums_ref[0:1, :] += jnp.sum(dhid * unit, axis=0, keepdims=True)
    sums_ref[1:2, :] += jnp.sum(dhid, axis=0, keepdims=True)
    dresid = cot.astype(f32) + norm_back(unit, scale, gains_ref[2:3, :], dhid)
    dresid_ref[...] = dresid
    dbranch = dresid.astype(bf16)
    dbranch_ref[...] = dbranch
    dmixed_all = dg(wout_ref[...], dbranch, 1, 1)
    for head in range(width // head_dim):
        low, high = (head * head_dim, (head + 1) * head_dim)
        dmixed = dmixed_all[low:high]
        inverse = inverse_ref[head : head + 1, :]
        dnum = dmixed * inverse
        dden = -jnp.sum(dmixed * mixed_ref[low:high, :], axis=0, keepdims=True) * inverse
        dnum_ref[low:high, :] = dnum
        dden_ref[head] = dden
        wide = stacked(*parts_of(dnum * opened), rows_of(parts_of(dden * opened), rows))
        local = dg(wide, pq_ref[2 * low : 2 * high, :], 1, 1)
        gstate_ref[low:high, :] += local[:head_dim] + local[head_dim:features]
        gnorm_ref[head : head + 1, :] += local[features : features + 1] + local[features + 1 : features + 2]

    @pl.when(pl.program_id(0) == pl.num_programs(0) - 1)
    def _():
        pack_carry(packed_ref, gstate_ref, gnorm_ref, last_start(starts_ref))


def logit_back(phi, dphi):
    half = phi.shape[0] // 2
    up, down = (phi[:half].astype(f32), phi[half:].astype(f32))
    dup, ddown = (dphi[:half], dphi[half:])
    dup = dup - jnp.sum(dup * up, axis=0, keepdims=True)
    ddown = ddown - jnp.sum(ddown * down, axis=0, keepdims=True)
    return (up * dup - down * ddown).astype(bf16)


def local_back_kernel(
    pq_ref, pk_ref, q_ref, v_ref, dnum_ref, dden_ref, start_ref, open_ref, state_ref, norm_ref, fq_ref,
    dq_ref, gfq_ref, dphik_ref, dv_ref,
):
    tokens = pq_ref.shape[1]
    features = pq_ref.shape[0]
    step = min(256, tokens)
    state_high, state_low = parts_of(state_ref[...])
    norm_high, norm_low = parts_of(norm_ref[0])
    carried = stacked(
        state_high, state_high, state_low, rows_of((norm_high, norm_high, norm_low), features)
    )
    maps = fq_ref[...]
    gfq = jnp.zeros(gfq_ref.shape[1:], f32)
    lows = list(range(0, tokens, step))

    def weights_at(low):
        high = low + step
        start = start_ref[:, low:high]
        phi = pq_ref[:, low:high]
        dnum_low = dnum_ref[:, low:high].astype(bf16)
        dden = dden_ref[0, :, low:high]
        plain = lambda first, last: dg(pk_ref[:, first:last], phi, 0, 0)
        slope = lambda first, last: dg(v_ref[:, first:last], dnum_low, 0, 0) + dden
        return causal(plain, start, low, high), causal(slope, start, low, high)

    upcoming = weights_at(lows[-1])
    for at in range(len(lows) - 1, -1, -1):
        low, high = (lows[at], lows[at] + step)
        weights, dweights = upcoming
        if at:
            upcoming = weights_at(lows[at - 1])
        phi = pq_ref[:, low:high]
        num_high, num_low = parts_of(dnum_ref[:, low:high])
        dden = dden_ref[0, :, low:high]
        dv = dg(num_high.astype(bf16), weights, 1, 1)
        dphik = dg(phi, dweights, 1, 1)
        if at == len(lows) - 1:
            dv_ref[...] = dv
            dphik_ref[...] = dphik
        else:
            dv_ref[:, :high] += dv
            dphik_ref[:, :high] += dphik
        den_high, den_low = parts_of(dden)
        arriving = stacked(num_high, num_low, num_high, rows_of((den_high, den_low, den_high), step))
        dphi = dg(pk_ref[:, :high], dweights, 1, 0)
        dphi = dphi + open_ref[:, low:high] * dg(carried, arriving, 0, 0)
        dlogit = logit_back(phi, dphi)
        gfq = gfq + dg(q_ref[:, low:high], dlogit, 1, 1)
        dq_ref[:, low:high] = dg(maps, dlogit, 1, 0).astype(bf16)
    gfq_ref[0] = gfq


def key_back_kernel(
    pk_ref, k_ref, v_ref, dphik0_ref, dphik1_ref, dv0_ref, dv1_ref, tail_ref, home_ref, fk_ref,
    dkv_ref, gfk_ref, state_ref, norm_ref,
):
    features, tokens = pk_ref.shape
    head_dim = features // 2
    head = pl.program_id(0)

    @pl.when(head == 0)
    def _():
        unpack_carry(home_ref, state_ref, norm_ref)

    first = pl.multiple_of(head * head_dim, head_dim)
    state_high, state_low = parts_of(state_ref[pl.ds(first, head_dim), :])
    carried = stacked(state_high, state_low, rows_of(parts_of(norm_ref[pl.ds(head, 1), :]), features))
    values = v_ref[...]
    tail = tail_ref[...]
    wide = stacked(values, values, jnp.ones((16, tokens), bf16))
    phi = pk_ref[...]
    early = pl.program_id(0) < pl.num_programs(0) // 2
    dphi = jnp.where(early, dphik0_ref[...], dphik1_ref[...]) + tail * dg(carried, wide, 0, 0)
    both = dg(stacked(state_high, state_low), phi, 1, 0)
    dv = jnp.where(early, dv0_ref[...], dv1_ref[...]) + tail * (both[:head_dim] + both[head_dim:])
    dlogit = logit_back(phi, dphi)
    gfk_ref[0] = dg(k_ref[...], dlogit, 1, 1)
    dkv_ref[0] = dg(fk_ref[...], dlogit, 1, 0).astype(bf16)
    dkv_ref[1] = dv.astype(bf16)


def leave_kernel(dq0_ref, dq1_ref, dkv_ref, w_ref, x_ref, gains_ref, dresid_ref, grad_ref, sums_ref):
    width = x_ref.shape[1]

    @pl.when(pl.program_id(0) == 0)
    def _():
        sums_ref[...] = jnp.zeros_like(sums_ref)

    dq = jnp.concatenate([dq0_ref[...], dq1_ref[...]], axis=0)
    dhid = dg(dq, w_ref[:, :width], 0, 1)
    dhid = dhid + dg(dkv_ref[0], w_ref[:, width : 2 * width], 0, 1)
    dhid = dhid + dg(dkv_ref[1], w_ref[:, 2 * width :], 0, 1)
    unit, scale = norm_parts(x_ref[...].astype(f32))
    sums_ref[0:1, :] += jnp.sum(dhid * unit, axis=0, keepdims=True)
    sums_ref[1:2, :] += jnp.sum(dhid, axis=0, keepdims=True)
    grad_ref[...] = dresid_ref[...] + norm_back(unit, scale, gains_ref[0:1, :], dhid)


def whole(shape):
    return pl.BlockSpec(shape, lambda i: (0,) * len(shape))


def down(rows, width):
    return pl.BlockSpec((rows, width), lambda i: (i, 0))


def across(rows, width):
    return pl.BlockSpec((rows, width), lambda i: (0, i))


def heads_across(heads, width):
    return pl.BlockSpec((heads, 1, width), lambda i: (0, 0, i))


def one_head(width, first=0):
    return pl.BlockSpec((1, 1, width), lambda i: (first + i, 0, 0))


def head_rows(rows, width, first=0):
    return pl.BlockSpec((rows, width), lambda i: (first + i, 0))


def shape_of(shape, dtype):
    return jax.ShapeDtypeStruct(shape, dtype)


def call(kernel, grid, ins, outs, shapes, args, scratch=()):
    return pl.pallas_call(
        kernel,
        grid=(grid,),
        in_specs=ins,
        out_specs=outs,
        out_shape=shapes,
        scratch_shapes=list(scratch),
        compiler_params=pltpu.CompilerParams(
            dimension_semantics=("arbitrary",), vmem_limit_bytes=grant
        ),
    )(*args)


def log2_of(count):
    return count.bit_length() - 1


def sizes():
    return (lax.axis_size("grp"), lax.axis_size("tok"))


def place_of():
    return lax.axis_index("grp") * lax.axis_size("tok") + lax.axis_index("tok")


def flips(first, second):
    grp_size, tok_size = sizes()
    pairs = []
    for place in range(grp_size * tok_size):
        pairs.append((place, place ^ (second if (place // tok_size) % 2 else first)))
    return pairs


def far_flips():
    grp_size, tok_size = sizes()
    return [(2 * tok_size) << bit for bit in range(log2_of(grp_size) - 1)]


def order_of(turn):
    tok_bits = [1 << bit for bit in range(log2_of(lax.axis_size("tok")))]
    near = far_flips() + tok_bits[:-1]
    turn = turn % len(near)
    return near[turn:] + near[:turn] + tok_bits[-1:]


def slots_of(turn):
    grp_size, tok_size = sizes()
    order = order_of(turn)
    slots = []
    for tok in range(tok_size):
        for far in range(grp_size // 2):
            place = far * 2 * tok_size + tok
            bits = [(place // flip) % 2 for flip in order]
            slots.append(sum(bit << (len(bits) - 1 - at) for at, bit in enumerate(bits)))
    return jnp.array(slots, jnp.int32)


def tables_of(turns):
    core = lax.axis_index("grp") % 2
    own = lax.axis_index("tok") * (lax.axis_size("grp") // 2) + lax.axis_index("grp") // 2
    even, odd = (slots_of(turns[0]), slots_of(turns[1]))
    mine = jnp.where(core == 0, even, odd)
    theirs = jnp.where(core == 0, odd, even)
    return jnp.concatenate([theirs ^ theirs[own], mine ^ mine[own], core[None].astype(jnp.int32)])


def product_kernel(counts, theirs, mine, last_forms, by_columns, table_ref, *refs):
    if last_forms is None:
        product_step(counts, theirs, mine, by_columns, table_ref, refs)
        return
    last = pl.num_programs(0) - 1

    @pl.when(pl.program_id(0) < last)
    def _():
        product_step(counts, theirs, mine, by_columns, table_ref, refs)

    @pl.when(pl.program_id(0) == last)
    def _():
        product_step(counts, *last_forms, by_columns, table_ref, refs)


def product_step(counts, theirs, mine, by_columns, table_ref, refs):
    count, tails = counts
    ins, refs = (refs[:count], refs[count:])
    tail_refs, refs = (refs[:tails], refs[tails:])
    theirs_ref, keep_ref, give_ref = refs
    pieces = (table_ref.shape[0] - 1) // 2
    half = pieces // 2
    rows, lanes = theirs_ref.shape[1:]
    for turn, forms in enumerate((theirs, mine)):
        at = 0
        blocks = []
        for left, right, left_dim, right_dim in forms:
            right = ins[right][...]
            value = dg(ins[left][...], right.reshape(right.shape[-2:]), left_dim, right_dim)
            blocks.append((at, value))
            at += value.shape[1]
        if tails:
            blocks.append((at, tail_refs[turn][0]))
        base = turn * pieces
        cuts = []
        for column, value in blocks:
            if by_columns:
                far = value.shape[0] // rows
                for tok in range(value.shape[1] // lanes):
                    for place in range(far):
                        part = value[place * rows : (place + 1) * rows, tok * lanes : (tok + 1) * lanes]
                        cuts.append((tok * far + place, slice(0, lanes), part))
                base = turn * pieces + pl.program_id(0) * len(cuts)
            else:
                for piece in range(value.shape[0] // rows):
                    part = value[piece * rows : (piece + 1) * rows]
                    cuts.append((piece, slice(column, column + value.shape[1]), part))
        for piece, span, part in cuts:
            slot = table_ref[base + piece]
            if turn == 0:
                theirs_ref[slot, :, span] = part
                continue

            @pl.when(slot < half)
            def _(part=part, span=span, slot=slot):
                keep_ref[slot, :, span] = part

            @pl.when(slot >= half)
            def _(part=part, span=span, slot=slot):
                give_ref[slot - half, :, span] = part


def products(table, theirs, mine, ins, specs, grid, piece, tail=None, by_columns=False, last=None):
    pieces = (table.shape[0] - 1) // 2
    if by_columns or grid == 1:
        block = lambda count: pl.BlockSpec((count,) + piece, lambda i, t: (0, 0, 0))
    else:
        block = lambda count: pl.BlockSpec((count, piece[0], piece[1] // grid), lambda i, t: (0, 0, i))
    specs = list(specs)
    ins = list(ins)
    count = len(ins)
    if tail is not None:
        ins += [tail, tail]
        specs.append(pl.BlockSpec((1,) + tail.shape[1:], lambda i, t: (1 - t[2 * pieces], 0, 0)))
        specs.append(pl.BlockSpec((1,) + tail.shape[1:], lambda i, t: (t[2 * pieces], 0, 0)))
    counts = (pieces, pieces // 2, pieces // 2)
    return pl.pallas_call(
        partial(product_kernel, (count, len(ins) - count), theirs, mine, last, by_columns),
        grid_spec=pltpu.PrefetchScalarGridSpec(
            num_scalar_prefetch=1, grid=(grid,), in_specs=specs, out_specs=[block(c) for c in counts]
        ),
        out_shape=[shape_of((c,) + piece, f32) for c in counts],
        compiler_params=pltpu.CompilerParams(
            dimension_semantics=("arbitrary",), vmem_limit_bytes=grant
        ),
    )(table, *ins)


def send(value, first, second):
    return lax.ppermute(value, ("grp", "tok"), flips(first, second))


def swap_cores(value):
    tok_size = lax.axis_size("tok")
    return send(value, tok_size, tok_size)


def fold(keep, give, other, turns):
    orders = (order_of(turns[0]), order_of(turns[1]))
    count = keep.shape[0]
    give = give + other[count:]
    other = other[:count]
    for at, (even, odd) in enumerate(zip(*orders)):
        landed = send(give, even, odd)
        half = keep.shape[0] // 2
        if at == 0:
            landed_of = lambda low, high: landed[low:high] + other[low:high]
        else:
            landed_of = lambda low, high: landed[low:high]
        if half:
            give = keep[half:] + landed_of(half, 2 * half)
            keep = keep[:half] + landed_of(0, half)
        else:
            keep = keep + landed_of(0, 1)
    for flip in far_flips():
        bit = (place_of() & flip) != 0
        landed = send(keep, flip, flip)
        keep = jnp.concatenate(
            [jnp.where(bit, landed, keep), jnp.where(bit, keep, landed)], axis=0
        )
    keep = keep.reshape(-1, keep.shape[2])
    landed = swap_cores(keep)
    core = lax.axis_index("grp") % 2
    return (jnp.where(core == 0, keep, landed), jnp.where(core == 0, landed, keep))


def chain_kernel(backward, got_ref, out_ref):
    count, rows, lanes = got_ref.shape

    def step(at, so_far):
        block = count - 1 - at if backward else at
        out_ref[block] = so_far
        local = got_ref[block]
        return local + local[rows - 1 :, :] * so_far

    lax.fori_loop(0, count, step, jnp.zeros((rows, lanes), f32), unroll=8)


def carry_scan(packed, backward):
    landed = lax.all_to_all(packed, ("grp", "tok"), 0, 0, tiled=True)
    summed = pl.pallas_call(
        partial(chain_kernel, backward),
        out_shape=shape_of(landed.shape, f32),
        compiler_params=pltpu.CompilerParams(vmem_limit_bytes=grant),
    )(landed)
    return lax.all_to_all(summed, ("grp", "tok"), 0, 0, tiled=True)


def reduce_vectors(stack):
    grp_size, tok_size = sizes()
    count, length = stack.shape
    share = length // tok_size
    blocks = stack.reshape(count, tok_size, share).transpose(1, 0, 2)
    blocks = blocks.reshape(tok_size, count * share)
    spread = jnp.broadcast_to(blocks[None], (grp_size,) + blocks.shape)
    spread = spread.reshape(grp_size * tok_size, count * share)
    landed = lax.all_to_all(spread, ("grp", "tok"), 0, 0, tiled=True)
    return jnp.sum(landed, axis=0).reshape(count, share)


def on_device(
    layer_input,
    doc_starts,
    ln1_gain,
    ln1_shift,
    w_qkv,
    feat_q,
    feat_k,
    w_out,
    ln2_gain,
    ln2_shift,
    w_fc,
    w_proj,
    cotangent,
):
    tokens, width = layer_input.shape
    head_dim = feat_q.shape[1]
    heads = width // head_dim
    feats = 2 * head_dim
    hidden = w_fc.shape[1]
    rows = min(256, tokens)
    blocks = tokens // rows
    gains = jnp.stack([ln1_gain, ln1_shift, ln2_gain, ln2_shift])

    at = jnp.arange(tokens, dtype=jnp.int32)
    marked = (doc_starts[:, None] > 0) & (at[:, None] <= at[None, :])
    last = jnp.max(jnp.where(marked, at[:, None], -1), axis=0)
    start = jnp.maximum(last, 0)[None]
    opened = (last < 0).astype(f32)[None]
    tail = (at >= last[-1]).astype(f32)[None]
    starts = doc_starts[None]
    grp_size, tok_size = sizes()
    count = grp_size * tok_size
    carry_shape = (count, width // count + 2, feats)
    carry_block = pl.BlockSpec(carry_shape, lambda i: (0, 0, 0))

    hid1, qkv, phi_q, phi_k, packed = call(
        enter_kernel, blocks,
        [down(rows, width), whole((4, width)), whole(w_qkv.shape),
         whole((head_dim, width)), whole((head_dim, width)), whole((1, tokens))],
        [across(width, rows), across(3 * width, rows), across(2 * width, rows), across(2 * width, rows),
         carry_block],
        [shape_of((width, tokens), bf16), shape_of((3 * width, tokens), bf16),
         shape_of((2 * width, tokens), bf16), shape_of((2 * width, tokens), bf16),
         shape_of(carry_shape, f32)],
        (layer_input, gains, w_qkv, feat_q.T, feat_k.T, starts),
        [pltpu.VMEM((2 * width, rows), f32), pltpu.VMEM((width, feats), f32), pltpu.VMEM((heads, feats), f32)],
    )
    home = carry_scan(packed, False)
    part = heads // 2
    locals_ = [
        call(
            local_kernel, part,
            [head_rows(feats, tokens, at * part), head_rows(feats, tokens, at * part),
             head_rows(head_dim, tokens, 2 * heads + at * part), whole((1, tokens))],
            [head_rows(head_dim, tokens), one_head(tokens)],
            [shape_of((width // 2, tokens), f32), shape_of((part, 1, tokens), f32)],
            (phi_q, phi_k, qkv, start),
        )
        for at in range(2)
    ]
    once = lambda shape: pl.BlockSpec(shape, lambda i: (0, 0), pipeline_mode=pl.Buffered(1))
    mixed_low, hid2, act, dpre, output, dbranch, dresid, dnum, dden, back_packed, sums2, state_in, norms_in = call(
        block_kernel, blocks,
        [across(width // 2, rows), across(width // 2, rows), heads_across(part, rows),
         heads_across(part, rows), across(2 * width, rows), carry_block,
         whole((1, tokens)), across(1, rows), down(rows, width), down(rows, width), whole((4, width)),
         once(w_out.shape), once(w_fc.shape), once(w_proj.shape)],
        [across(width, rows), across(width, rows), down(rows, hidden), down(rows, hidden),
         down(rows, width), down(rows, width), down(rows, width), across(width, rows),
         heads_across(heads, rows), carry_block, whole((8, width)), whole((width, feats)),
         whole((heads, 1, feats))],
        [shape_of((width, tokens), bf16), shape_of((width, tokens), bf16), shape_of((tokens, hidden), bf16),
         shape_of((tokens, hidden), bf16), shape_of((tokens, width), bf16), shape_of((tokens, width), bf16),
         shape_of((tokens, width), f32), shape_of((width, tokens), f32), shape_of((heads, 1, tokens), f32),
         shape_of(carry_shape, f32), shape_of((8, width), f32), shape_of((width, feats), f32),
         shape_of((heads, 1, feats), f32)],
        (locals_[0][0], locals_[1][0], locals_[0][1], locals_[1][1], phi_q, home, starts, opened,
         layer_input, cotangent, gains, w_out, w_fc, w_proj),
        [pltpu.VMEM((width, rows), f32), pltpu.VMEM((16, rows), f32), pltpu.VMEM((heads, feats), f32),
         pltpu.VMEM((width, feats), f32), pltpu.VMEM((heads, feats), f32)],
    )
    half = width // 2
    fars, toks = (lax.axis_size("grp") // 2, lax.axis_size("tok"))
    piece_rows = width // (fars * toks)
    turns_a, turns_b, turns_c, turns_d = ((0, 1), (2, 0), (2, 0), (0, 1))
    table_a, table_b, table_c, table_d = map(tables_of, (turns_a, turns_b, turns_c, turns_d))
    last_at = table_a.shape[0] - 1
    plain = lambda rows_: pl.BlockSpec((rows_, tokens), lambda i, t: (0, 0))
    which = lambda turn, t: t[last_at] if turn else 1 - t[last_at]
    right_half = lambda turn: pl.BlockSpec((tokens, half), lambda i, t: (0, which(turn, t)))
    chosen = lambda row, turn: pl.BlockSpec((1, half, tokens), lambda i, t: (row, which(turn, t), 0))
    quarter = lambda turn: pl.BlockSpec(
        (tokens, half), lambda i, t: (0, hidden // width * which(turn, t) + jnp.minimum(i, hidden // width - 1))
    )
    theirs_a, keep_a, give_a = products(
        table_a, ((0, 2, 0, 0),), ((1, 2, 0, 0),), (cotangent, cotangent, act),
        (right_half(0), right_half(1), pl.BlockSpec((tokens, hidden // 4), lambda i, t: (0, i))),
        4, (half // fars, hidden // toks), None, True,
    )
    other_a = swap_cores(theirs_a)
    theirs_b, keep_b, give_b = products(
        table_b, ((0, 1, 1, 0),), ((0, 2, 1, 0),),
        (hid2, dpre, dpre, mixed_low, dbranch, dbranch),
        (plain(width), quarter(0), quarter(1), plain(width), right_half(0), right_half(1)),
        hidden // width + 1, (piece_rows, hidden // 2 + half),
        last=(((3, 4, 1, 0),), ((3, 5, 1, 0),)),
    )
    other_b = swap_cores(theirs_b)
    returned = carry_scan(back_packed, True)
    split = [
        call(
            local_back_kernel, part,
            [head_rows(feats, tokens, at * part), head_rows(feats, tokens, at * part),
             head_rows(head_dim, tokens, at * part), head_rows(head_dim, tokens, 2 * heads + at * part),
             head_rows(head_dim, tokens, at * part), one_head(tokens, at * part),
             whole((1, tokens)), whole((1, tokens)), head_rows(head_dim, feats, at * part),
             one_head(feats, at * part), head_rows(head_dim, head_dim, at * part)],
            [head_rows(head_dim, tokens), pl.BlockSpec((1, head_dim, head_dim), lambda i: (i, 0, 0)),
             head_rows(feats, tokens), head_rows(head_dim, tokens)],
            [shape_of((width // 2, tokens), bf16), shape_of((part, head_dim, head_dim), f32),
             shape_of((width, tokens), f32), shape_of((width // 2, tokens), f32)],
            (phi_q, phi_k, qkv, qkv, dnum, dden, start, opened, state_in, norms_in, feat_q),
        )
        for at in range(2)
    ]
    gfq = jnp.concatenate([split[0][1], split[1][1]], axis=0)
    lower = lambda rows_: pl.BlockSpec((rows_, tokens), lambda i: (jnp.minimum(i, part - 1), 0))
    upper = lambda rows_: pl.BlockSpec((rows_, tokens), lambda i: (jnp.maximum(i - part, 0), 0))
    dkv, gfk = call(
        key_back_kernel, heads,
        [head_rows(feats, tokens), head_rows(head_dim, tokens, heads),
         head_rows(head_dim, tokens, 2 * heads), lower(feats), upper(feats), lower(head_dim), upper(head_dim),
         whole((1, tokens)), carry_block, head_rows(head_dim, head_dim)],
        [pl.BlockSpec((2, head_dim, tokens), lambda i: (0, i, 0)),
         pl.BlockSpec((1, head_dim, head_dim), lambda i: (i, 0, 0))],
        [shape_of((2, width, tokens), bf16), shape_of((heads, head_dim, head_dim), f32)],
        (phi_k, qkv, qkv, split[0][2], split[1][2], split[0][3], split[1][3], tail, returned, feat_k),
        [pltpu.VMEM((width, feats), f32), pltpu.VMEM((heads, feats), f32)],
    )
    grad_input, sums1 = call(
        leave_kernel, blocks,
        [across(width // 2, rows), across(width // 2, rows),
         pl.BlockSpec((2, width, rows), lambda i: (0, 0, i)), whole(w_qkv.shape),
         down(rows, width), whole((4, width)), down(rows, width)],
        [down(rows, width), whole((8, width))],
        [shape_of((tokens, width), f32), shape_of((8, width), f32)],
        (split[0][0], split[1][0], dkv, w_qkv, layer_input, gains, dresid),
    )

    first_core = lax.axis_index("grp") % 2 == 0
    theirs_q = jnp.where(first_core, split[1][0], split[0][0])
    mine_q = jnp.where(first_core, split[0][0], split[1][0])
    theirs_c, keep_c, give_c = products(
        table_c, ((0, 1, 1, 1),), ((0, 2, 1, 1),), (hid1, theirs_q, mine_q),
        (plain(width), plain(half), plain(half)), 1, (piece_rows, half),
    )
    other_c = swap_cores(theirs_c)
    feats_both = jnp.stack([gfq.reshape(width, head_dim), gfk.reshape(width, head_dim)])
    feats_both = jnp.pad(feats_both, ((0, 0), (0, 0), (0, feats - head_dim)))

    theirs_d, keep_d, give_d = products(
        table_d, ((0, 1, 1, 1), (0, 2, 1, 1)), ((0, 3, 1, 1), (0, 4, 1, 1)),
        (hid1, dkv, dkv, dkv, dkv),
        (plain(width), chosen(0, 0), chosen(1, 0), chosen(0, 1), chosen(1, 1)),
        1, (piece_rows, 2 * half + feats), feats_both,
    )
    other_d = swap_cores(theirs_d)
    vectors = reduce_vectors(jnp.concatenate([sums1[:2], sums2[:2]], axis=0))
    a_pair = fold(keep_a, give_a, other_a, turns_a)
    b_pair = fold(keep_b, give_b, other_b, turns_b)
    c_pair = fold(keep_c, give_c, other_c, turns_c)
    d_pair = fold(keep_d, give_d, other_d, turns_d)
    inner = hidden // 2
    grad_proj = jnp.concatenate(a_pair, axis=0).T
    grad_fc = jnp.concatenate([part[:, :inner] for part in b_pair], axis=1)
    grad_out = jnp.concatenate([part[:, inner:] for part in b_pair], axis=1)
    grad_qkv = jnp.concatenate(
        list(c_pair)
        + [part[:, :half] for part in d_pair]
        + [part[:, half : 2 * half] for part in d_pair],
        axis=1,
    )
    return (
        output,
        grad_input,
        vectors[0],
        vectors[1],
        grad_qkv,
        d_pair[0][:, 2 * half : 2 * half + head_dim],
        d_pair[1][:, 2 * half : 2 * half + head_dim],
        grad_out,
        vectors[2],
        vectors[3],
        grad_fc,
        grad_proj,
    )


def solution(mesh):
    in_specs = (
        P(("grp", "tok"), None),
        P(("grp", "tok")),
        P(),
        P(),
        P(),
        P(),
        P(),
        P(),
        P(),
        P(),
        P(),
        P(),
        P(("grp", "tok"), None),
    )
    out_specs = (
        P(("grp", "tok"), None),
        P(("grp", "tok"), None),
        P("tok"),
        P("tok"),
        P("tok", None),
        P("tok", None),
        P("tok", None),
        P("tok", None),
        P("tok"),
        P("tok"),
        P("tok", None),
        P("tok", None),
    )

    return jax.shard_map(on_device, mesh=mesh, in_specs=in_specs, out_specs=out_specs, check_vma=False)
```
